32 devices in a mesh: cuts: 8 (over z, core), tile: 4 (over y, x).
Axes of the slice: x: 2, y: 2, z: 4, core: 2. Of those that a mesh axis runs over, the one named last changes fastest.
Arguments:
- object_slices: float32 [8, 2, 768, 512], P('cuts', None, None, 'tile'), may hold values from -1.25 to 1.25, as said below
- probe_modes: float32 [4, 2, 128, 128], replicated, may hold values from -3 to 3
- prop_phase: float32 [128, 128], replicated, may hold values from -3.140625 to 3.140625
- measured: float32 [16, 128, 128], P('tile'), may hold values from 0 to 4
- row_offsets: int32 [16], P('tile'), may hold values from 0 to 640
- col_offsets: int32 [16], P('tile'), may hold values from 0 to 127
- counts: int32 [4], P('tile'), may hold values from 1 to 4, 12 in all
Outputs:
- object_grad: float32 [8, 2, 768, 512], P('cuts', None, None, 'tile')
The draws below stay inside these ranges and needn't reach their ends.
Inputs may be any that keep to these rules, and one draw needn't show every extreme that they name: `counts`: every group of 4 slots holds at least one window, and some group is full in every draw. `object_slices`: each pixel's transmission has a magnitude between 0.8 and 1.25.
All inputs are finite; a program needn't handle non-finite values.
Results may differ from the reference program's by a relative error of at most 0.03.
Values may be sent and summed in bfloat16 or wider, within the bound.
No kernel may reach another device: no remote copies, remote signals or barrier semaphores. Data moves between devices by JAX's collectives and lax.ppermute only.
A program may use at most 64 MiB of HBM per device.

```python
import math
import jax
import jax.numpy as jnp
import numpy as np
from jax import lax

WIN = 128
MODES = 4
ROWS = 768
P_MAX = 4
SLICES = 8
COLS = 512
POSITIONS = 16
N_TILE = 4


def draw_object_slices(key, part):
    amp_key = jax.random.fold_in(key, 11)
    phase_key = jax.random.fold_in(key, 12)
    shape = (SLICES, ROWS, COLS)
    magnitude = jnp.exp(jax.random.uniform(amp_key, shape, jnp.float32, math.log(0.8), math.log(1.25)))
    phase = jax.random.uniform(phase_key, shape, jnp.float32, -math.pi, math.pi)
    return jnp.stack([magnitude * jnp.cos(phase), magnitude * jnp.sin(phase)], axis=1).astype(jnp.float32)


def place_ends(result, key, least, top_value):
    place = [jax.random.randint(jax.random.fold_in(key, axis), (), 0, length) for axis, length in enumerate(result.shape)]
    widest = result.shape.index(max(result.shape))
    beside = place[:widest] + [(place[widest] + 1) % result.shape[widest]] + place[widest + 1:]
    return result.at[tuple(place)].set(least).at[tuple(beside)].set(top_value)


def block_scale(key, shape, cuts, smallest, high):
    level, own = 1.0, jax.random.fold_in(key, 6)
    for position, blocks in cuts:
        steps = jnp.exp(jax.random.uniform(jax.random.fold_in(own, position), (blocks,), jnp.float32, smallest / len(cuts), high / len(cuts)))
        level = level * jnp.repeat(steps, shape[position] // blocks).reshape([-1 if axis == position else 1 for axis in range(len(shape))])
    return level


def length_profile(amount, total, reach, slope):
    weights = [(1 << 20) // math.isqrt(grade ** slope) + 1 for grade in range(2, amount + 1)]
    rest, given = total - reach - (amount - 1), [1] * (amount - 1)
    while rest > 0:
        movable = [i for i in range(amount - 1) if given[i] < reach]
        mass, budget = sum([weights[i] for i in movable]), rest
        for i in movable:
            more = min(reach - given[i], max(1, budget * weights[i] // mass), rest)
            given[i] = given[i] + more
            rest = rest - more
    return np.array([reach] + given)


def ragged_sizes(own_key, number_of, total, limit, lean):
    if number_of == 2:
        one = jax.random.randint(own_key, (), max(1, total - limit), min(limit, total - 1) + 1)
        return jnp.stack([one, total - one])
    lengths = jnp.asarray(length_profile(number_of, total, limit, lean), jnp.int32)
    couples = (number_of - 1) // 2
    giver, receiver = lengths[1:1 + 2 * couples:2], lengths[2:2 + 2 * couples:2]
    margin = jnp.minimum(giver - 1, limit - receiver)
    shifted = jax.random.randint(jax.random.fold_in(own_key, 1), (couples,), 0, 1 << 20) % (margin + 1)
    lengths = lengths.at[1:1 + 2 * couples:2].set(giver - shifted).at[2:2 + 2 * couples:2].set(receiver + shifted)
    return lengths[jax.random.permutation(jax.random.fold_in(own_key, 2), number_of)]


def bell_draw(own_key, shape, width, limit, kind=jnp.bfloat16):
    drawn = width * jax.random.normal(own_key, shape, jnp.float32)
    return jnp.clip(drawn, min=-limit, max=limit).astype(kind)


def setup_inputs(seed: int = 0) -> dict:
    streams_of = jax.random.split(jax.random.key(seed), 8)
    object_slices = draw_object_slices(jax.random.fold_in(streams_of[7], 71), 0)
    probe_modes = bell_draw(streams_of[1], (MODES, 2, WIN, WIN), 0.5, 3.0, jnp.float32)
    prop_phase = jnp.clip(jax.random.uniform(streams_of[2], (WIN, WIN), jnp.float32, -3.140625, 3.140625), -3.140625, 3.140625)
    measured = jnp.clip(4.0 * jax.random.uniform(streams_of[3], (POSITIONS, WIN, WIN), jnp.float32) ** block_scale(streams_of[3], (POSITIONS, WIN, WIN), ((0, 4),), -0.2, 0.2), 0.0, 4.0)
    row_offsets = place_ends(jax.random.randint(streams_of[4], (POSITIONS,), 0, ROWS - WIN + 1), jax.random.fold_in(streams_of[4], 1), 0, ROWS - WIN).astype(jnp.int32)
    col_offsets = place_ends(jax.random.randint(streams_of[5], (POSITIONS,), 0, WIN), jax.random.fold_in(streams_of[5], 1), 0, WIN - 1).astype(jnp.int32)
    counts = ragged_sizes(streams_of[6], N_TILE, N_TILE * P_MAX * 3 // 4, P_MAX, 2).astype(jnp.int32)
    return {"object_slices": object_slices, "probe_modes": probe_modes, "prop_phase": prop_phase, "measured": measured, "row_offsets": row_offsets, "col_offsets": col_offsets, "counts": counts}


HIGHEST = lax.Precision.HIGHEST

def dft_tables(win_size):
    numbers = jnp.arange(win_size, dtype=jnp.int32)
    angles = (numbers[:, None] * numbers[None, :] % win_size).astype(jnp.float32) * (2.0 * math.pi / win_size)
    factor = 1.0 / math.sqrt(win_size)
    return (jnp.cos(angles) * factor, jnp.sin(angles) * factor)

def left_mul(mat_real, mat_imag, real_part, imag_part):
    real_real = jnp.einsum('jk,...kl->...jl', mat_real, real_part, precision=HIGHEST)
    imag_imag = jnp.einsum('jk,...kl->...jl', mat_imag, imag_part, precision=HIGHEST)
    real_imag = jnp.einsum('jk,...kl->...jl', mat_real, imag_part, precision=HIGHEST)
    imag_real = jnp.einsum('jk,...kl->...jl', mat_imag, real_part, precision=HIGHEST)
    return (real_real - imag_imag, real_imag + imag_real)

def right_mul(real_part, imag_part, mat_real, mat_imag):
    real_real = jnp.einsum('...jk,kl->...jl', real_part, mat_real, precision=HIGHEST)
    imag_imag = jnp.einsum('...jk,kl->...jl', imag_part, mat_imag, precision=HIGHEST)
    real_imag = jnp.einsum('...jk,kl->...jl', real_part, mat_imag, precision=HIGHEST)
    imag_real = jnp.einsum('...jk,kl->...jl', imag_part, mat_real, precision=HIGHEST)
    return (real_real - imag_imag, real_imag + imag_real)

def transform(real_part, imag_part, cosine, sine_table, forward):
    signed = -sine_table if forward else sine_table
    real_part, imag_part = left_mul(cosine, signed, real_part, imag_part)
    return right_mul(real_part, imag_part, cosine, signed)

def complex_mul(a_real, a_imag, b_real, b_imag):
    return (a_real * b_real - a_imag * b_imag, a_real * b_imag + a_imag * b_real)

def propagate(real_part, imag_part, phase_cos, phase_sin, cosine, sine_table):
    freq_real, freq_imag = transform(real_part, imag_part, cosine, sine_table, True)
    freq_real, freq_imag = complex_mul(phase_cos, phase_sin, freq_real, freq_imag)
    return transform(freq_real, freq_imag, cosine, sine_table, False)

def section_forward(incoming, patch_now, phase_cos, phase_sin, cosine, sine_table):
    wave_real = incoming[:, 0].astype(jnp.float32)
    wave_imag = incoming[:, 1].astype(jnp.float32)
    prod_real, prod_imag = complex_mul(wave_real, wave_imag, patch_now[0], patch_now[1])
    out_real, out_imag = propagate(prod_real, prod_imag, phase_cos, phase_sin, cosine, sine_table)
    return jnp.stack([out_real, out_imag], axis=1).astype(jnp.bfloat16)

def loss_back(incoming, patch_now, target, weight, cosine, sine_table):
    wave_real = incoming[:, 0].astype(jnp.float32)
    wave_imag = incoming[:, 1].astype(jnp.float32)
    prod_real, prod_imag = complex_mul(wave_real, wave_imag, patch_now[0], patch_now[1])
    det_real, det_imag = transform(prod_real, prod_imag, cosine, sine_table, True)
    intensity = lax.optimization_barrier(jnp.sum(det_real * det_real + det_imag * det_imag, axis=0))
    factor = weight * (intensity - target) * 0.25
    return transform(factor * det_real, factor * det_imag, cosine, sine_table, False)

def adjoint_back(returned, phase_cos, phase_sin, cosine, sine_table):
    real_part = returned[:, 0].astype(jnp.float32)
    imag_part = returned[:, 1].astype(jnp.float32)
    return propagate(real_part, imag_part, phase_cos, -phase_sin, cosine, sine_table)

def patch_grad(incoming, back_pair):
    wave_real = incoming[:, 0].astype(jnp.float32)
    wave_imag = incoming[:, 1].astype(jnp.float32)
    back_real, back_imag = back_pair
    grad_real = lax.optimization_barrier(jnp.sum(wave_real * back_real + wave_imag * back_imag, axis=0))
    grad_imag = lax.optimization_barrier(jnp.sum(wave_real * back_imag - wave_imag * back_real, axis=0))
    return jnp.stack([grad_real, grad_imag], axis=0)

def wave_grad(patch_now, back_pair):
    back_real, back_imag = back_pair
    ret_real = patch_now[0] * back_real + patch_now[1] * back_imag
    ret_imag = patch_now[0] * back_imag - patch_now[1] * back_real
    return jnp.stack([ret_real, ret_imag], axis=1).astype(jnp.bfloat16)

def window_grads(patches, target, weight, probe_modes, phase_cos, phase_sin, cosine, sine_table):
    wave_now = probe_modes.astype(jnp.bfloat16)
    wave_list = []
    for slice_id in range(SLICES):
        wave_list.append(wave_now)
        if slice_id + 1 < SLICES:
            wave_now = section_forward(wave_now, patches[slice_id], phase_cos, phase_sin, cosine, sine_table)
    back_pair = loss_back(wave_list[-1], patches[-1], target, weight, cosine, sine_table)
    grad_slices = [None] * SLICES
    for slice_id in reversed(range(SLICES)):
        grad_slices[slice_id] = patch_grad(wave_list[slice_id], back_pair)
        if slice_id > 0:
            returned = wave_grad(patches[slice_id], back_pair)
            back_pair = adjoint_back(returned, phase_cos, phase_sin, cosine, sine_table)
    return jnp.stack(grad_slices, axis=0)

def reference(object_slices, probe_modes, prop_phase, measured, row_offsets, col_offsets, counts):
    cosine, sine_table = dft_tables(WIN)
    phase_cos = jnp.cos(prop_phase)
    phase_sin = jnp.sin(prop_phase)
    padded = jnp.pad(object_slices, ((0, 0), (0, 0), (0, 0), (0, WIN)))
    window_ids = jnp.arange(POSITIONS, dtype=jnp.int32)
    owner_ids = window_ids // P_MAX
    valid_flags = (window_ids % P_MAX < counts[owner_ids]).astype(jnp.float32)
    columns = (owner_ids * WIN + col_offsets).astype(jnp.int32)
    anchor = jnp.zeros((), jnp.int32)

    def add_window(canvas, window_item):
        row_at, col_at, target, weight = window_item
        start = (anchor, anchor, row_at.astype(jnp.int32), col_at.astype(jnp.int32))
        patches = lax.dynamic_slice(padded, start, (SLICES, 2, WIN, WIN))
        grads = window_grads(patches, target, weight, probe_modes, phase_cos, phase_sin, cosine, sine_table)
        current = lax.dynamic_slice(canvas, start, (SLICES, 2, WIN, WIN))
        return (lax.dynamic_update_slice(canvas, current + grads, start), None)
    canvas, _ = lax.scan(add_window, jnp.zeros_like(padded), (row_offsets.astype(jnp.int32), columns, measured, valid_flags))
    return canvas[:, :, :, :COLS]
```

```python
import functools
import math

import jax
import jax.numpy as jnp
import numpy as np
from jax import lax
from jax.experimental import pallas as pl
from jax.experimental.pallas import tpu as pltpu
from jax.sharding import PartitionSpec as P

F32 = jnp.float32
BF16 = jnp.bfloat16
CORES = 2
ENTRY_SCALE = 1.62475

VMEM = pl.BlockSpec(memory_space=pltpu.VMEM)
SMEM = pl.BlockSpec(memory_space=pltpu.SMEM)


def passed_along(block, axis, distance):
    devices = range(lax.axis_size(axis))
    route = [(i - distance, i) for i in devices if i - distance in devices]
    return lax.ppermute(block, axis, route)


def rotated(block, distance):
    size = lax.axis_size("cuts")
    return lax.ppermute(block, "cuts", [(i, (i + distance) % size) for i in range(size)])


def swapped(block):
    size = lax.axis_size("cuts")
    return lax.ppermute(block, "cuts", [(i, i ^ 1) for i in range(size)])


def dft_blocks(win):
    numbers = np.arange(win)
    angles = (numbers[:, None] * numbers[None, :] % win) * (2.0 * math.pi / win)
    cosine, sine = np.cos(angles) * ENTRY_SCALE, np.sin(angles) * ENTRY_SCALE
    return np.block([[cosine, sine], [-sine, cosine]]).astype(np.float32)


def rolled_rows(strip_ref, part, row_at, win, rows_mask_from):
    last = strip_ref.shape[1] // win - 1
    block = row_at // win
    upper = strip_ref[part, pl.ds(pl.multiple_of(block * win, win), win), :]
    after = jnp.minimum(block + 1, last)
    lower = strip_ref[part, pl.ds(pl.multiple_of(after * win, win), win), :]
    return jnp.where(rows_mask_from >= row_at - block * win, upper, lower)


def rows_kernel(chips, slots, win, chip_ref, rows_ref, strip_ref, *out_refs):
    row_ids = lax.broadcasted_iota(jnp.int32, (win, win), 0)
    for r in range(chips):
        slot = lax.rem(chip_ref[0] + r, chips) // (chips // slots)
        row_at = rows_ref[slot]
        for part in range(2):
            out_refs[r][part] = rolled_rows(strip_ref, part, row_at, win, row_ids).astype(BF16)


def rolled_probe_kernel(win, place_ref, probe_ref, out_ref):
    row_at, col_at = lax.rem(place_ref[0], win), place_ref[1]
    for mode in range(probe_ref.shape[0]):
        for part in range(2):
            block = pltpu.roll(probe_ref[mode, part], row_at, 0)
            out_ref[mode, part] = pltpu.roll(block, col_at, 1).astype(BF16)


def window_kernel(chips, modes, win, *refs):
    slices = CORES * chips
    (ints_ref, weight_ref, left_ref, right_ref, probe_ref, hcos_ref, hsin_ref, target_ref) = refs[:8]
    own_refs = refs[8 : 8 + chips]
    other_refs = refs[8 + chips : 8 + 2 * chips]
    out_refs = refs[8 + 2 * chips : 8 + 3 * chips]
    patch_ref, wave_ref, grad_ref = refs[8 + 3 * chips :]
    chip, core = ints_ref[0], ints_ref[1]
    unit = 1.0 / (ENTRY_SCALE * ENTRY_SCALE * win)
    for r in range(chips):
        source = lax.rem(chip - r + chips, chips)
        patch_ref[CORES * source + core] = own_refs[r][...]
        patch_ref[CORES * source + 1 - core] = other_refs[r][...]

    def from_left(matrix, pairs):
        stacked = jnp.concatenate(
            [jnp.concatenate([pair[k].astype(BF16) for pair in pairs], 1) for k in range(2)], 0
        )
        prod = jnp.dot(matrix, stacked, preferred_element_type=F32)
        return [
            (prod[:win, m * win : (m + 1) * win], prod[win:, m * win : (m + 1) * win])
            for m in range(modes)
        ]

    def from_right(pairs, matrix):
        stacked = jnp.concatenate(
            [jnp.concatenate([pair[k].astype(BF16) for k in range(2)], 1) for pair in pairs], 0
        )
        prod = jnp.dot(stacked, matrix, preferred_element_type=F32)
        return [
            (prod[m * win : (m + 1) * win, :win], prod[m * win : (m + 1) * win, win:])
            for m in range(modes)
        ]

    def transform(pairs):
        return from_right(from_left(left_ref[...], pairs), right_ref[...])

    def inverse(pairs):
        return from_right(from_left(right_ref[...], pairs), left_ref[...])

    def mul(a, b):
        return (a[0] * b[0] - a[1] * b[1], a[0] * b[1] + a[1] * b[0])

    def conj_mul(a, b):
        return (a[0] * b[0] + a[1] * b[1], a[0] * b[1] - a[1] * b[0])

    def patch_at(s):
        return (patch_ref[s, 0].astype(F32), patch_ref[s, 1].astype(F32))

    def waves_at(s):
        return [(wave_ref[s, m, 0], wave_ref[s, m, 1]) for m in range(modes)]

    def propagator():
        return (hcos_ref[...], hsin_ref[...])

    for m in range(modes):
        for part in range(2):
            wave_ref[0, m, part] = probe_ref[m, part].astype(F32)

    def forward_step(s, carry):
        patch = patch_at(s)
        freq = transform([mul(wave, patch) for wave in waves_at(s)])
        spread = propagator()
        waves = inverse([mul(spread, pair) for pair in freq])
        for m in range(modes):
            for part in range(2):
                wave_ref[s + 1, m, part] = waves[m][part]
        return carry

    lax.fori_loop(0, slices - 1, forward_step, 0)
    patch = patch_at(slices - 1)
    exits = transform([mul(wave, patch) for wave in waves_at(slices - 1)])
    power = sum(pair[0] * pair[0] + pair[1] * pair[1] for pair in exits) * (unit * unit)
    factor = (power - target_ref[...]) * (weight_ref[0] * (0.25 * unit * unit))
    back = inverse([(factor * pair[0], factor * pair[1]) for pair in exits])

    def keep_grad(s, back):
        grads = [conj_mul(wave, pair) for wave, pair in zip(waves_at(s), back)]
        for part in range(2):
            grad_ref[s, part] = sum(grad[part] for grad in grads).astype(BF16)

    keep_grad(slices - 1, back)

    def backward_step(i, back):
        s = slices - 1 - i
        patch = patch_at(s)
        freq = transform([conj_mul(patch, pair) for pair in back])
        spread = propagator()
        back = inverse([conj_mul(spread, pair) for pair in freq])
        keep_grad(s - 1, back)
        return back

    lax.fori_loop(0, slices - 1, backward_step, back)
    for r in range(chips):
        dest = lax.rem(chip + r, chips)
        out_refs[r][...] = grad_ref[CORES * dest + core]


def place_kernel(chips, slots, win, from_left, *refs):
    chip_ref, rows_ref, cols_ref = refs[:3]
    block_refs = refs[3 : 3 + chips]
    out_ref = refs[-1]
    if from_left:
        out_ref[...] = refs[3 + chips][...]
    else:
        out_ref[...] = jnp.zeros_like(out_ref)
    row_ids = lax.broadcasted_iota(jnp.int32, (win, win), 0)
    col_ids = lax.broadcasted_iota(jnp.int32, (win, win), 1)
    last = out_ref.shape[1] // win - 1
    copies = chips // slots
    for r in range(chips):
        source = lax.rem(chip_ref[0] - r + chips, chips)
        slot = source // copies
        row_at, col_at = rows_ref[slot], cols_ref[slot]
        mine = (col_ids < col_at) if from_left else (col_ids >= col_at)
        counted = lax.rem(source, copies) == 0
        block = row_at // win
        after = jnp.minimum(block + 1, last)
        upper = row_ids >= row_at - block * win
        for part in range(2):
            grad = jnp.where(mine & counted, block_refs[r][part].astype(F32), 0.0)
            at = pl.ds(pl.multiple_of(block * win, win), win)
            out_ref[part, at, :] = out_ref[part, at, :] + jnp.where(upper, grad, 0.0)
            at = pl.ds(pl.multiple_of(after * win, win), win)
            out_ref[part, at, :] = out_ref[part, at, :] + jnp.where(upper, 0.0, grad)


def local(object_slices, probe_modes, prop_phase, measured, row_offsets, col_offsets, counts):
    modes, _, win, _ = probe_modes.shape
    slots = row_offsets.shape[0]
    chips = lax.axis_size("cuts") // CORES
    copies = chips // slots
    assert chips % slots == 0
    section = lax.axis_index("cuts")
    chip, core = section // CORES, section % CORES
    strip = object_slices[0]
    block = jax.ShapeDtypeStruct((2, win, win), BF16)

    left_places = passed_along(jnp.concatenate([row_offsets, col_offsets]), "tile", 1)
    left_rows, left_cols = left_places[:slots], left_places[slots:]
    chip_one = jnp.reshape(chip, (1,)).astype(jnp.int32)

    select_rows = pl.pallas_call(
        functools.partial(rows_kernel, chips, slots, win),
        out_shape=[block] * chips,
        in_specs=[SMEM, SMEM, VMEM],
        out_specs=[VMEM] * chips,
    )
    own_rows = select_rows(chip_one, row_offsets, strip)
    slot = chip // copies
    place = jnp.stack([row_offsets[slot], col_offsets[slot]])
    probe = pl.pallas_call(
        functools.partial(rolled_probe_kernel, win),
        out_shape=jax.ShapeDtypeStruct(probe_modes.shape, BF16),
        in_specs=[SMEM, VMEM],
        out_specs=VMEM,
    )(place, probe_modes)
    matrix = dft_blocks(win)
    left_matrix = jnp.asarray(matrix, BF16)
    right_matrix = jnp.asarray(matrix.T, BF16)
    unit = 1.0 / (ENTRY_SCALE * ENTRY_SCALE * win)
    hcos = jnp.cos(prop_phase) * (unit * unit)
    hsin = jnp.sin(prop_phase) * (unit * unit)
    target = lax.dynamic_index_in_dim(measured, slot, 0, keepdims=False)
    weight = (slot < counts).astype(F32)
    ints = jnp.stack([chip, core]).astype(jnp.int32)

    beside_rows = select_rows(chip_one, left_rows, strip)
    own_blocks, other_blocks = [None] * chips, [None] * chips
    col_ids = lax.broadcasted_iota(jnp.int32, (2, win, win), 2)
    for r in list(range(1, chips)) + [0]:
        arrived = passed_along(beside_rows[r], "tile", -1)
        col_at = col_offsets[(chip + r) % chips // copies]
        merged = jnp.where(col_ids >= col_at, own_rows[r], arrived)
        own_blocks[r] = rotated(merged, CORES * r) if r else merged
        other_blocks[r] = swapped(own_blocks[r])

    grads = pl.pallas_call(
        functools.partial(window_kernel, chips, modes, win),
        out_shape=[block] * chips,
        in_specs=[SMEM, SMEM] + [VMEM] * (6 + 2 * chips),
        out_specs=[VMEM] * chips,
        scratch_shapes=[
            pltpu.VMEM((CORES * chips, 2, win, win), BF16),
            pltpu.VMEM((CORES * chips, modes, 2, win, win), F32),
            pltpu.VMEM((CORES * chips, 2, win, win), BF16),
        ],
        compiler_params=pltpu.CompilerParams(vmem_limit_bytes=48 * 2**20),
    )(ints, weight, left_matrix, right_matrix, probe, hcos, hsin, target, *own_blocks, *other_blocks)

    mine, wrapped = [], []
    for r in range(chips):
        arrived = rotated(grads[r], CORES * r) if r else grads[r]
        mine.append(arrived)
        wrapped.append(passed_along(arrived, "tile", 1))

    def placed(from_left, rows, cols, *arrays):
        return pl.pallas_call(
            functools.partial(place_kernel, chips, slots, win, from_left),
            out_shape=jax.ShapeDtypeStruct(strip.shape, F32),
            in_specs=[SMEM, SMEM, SMEM] + [VMEM] * len(arrays),
            out_specs=VMEM,
            input_output_aliases={3 + chips: 0} if from_left else {},
        )(chip_one, rows, cols, *arrays)

    own_part = placed(False, row_offsets, col_offsets, *mine)
    return placed(True, left_rows, left_cols, *wrapped, own_part)[None]


def solution(mesh):
    placed = (
        P("cuts", None, None, "tile"),
        P(),
        P(),
        P("tile", None, None),
        P("tile"),
        P("tile"),
        P("tile"),
    )
    return jax.shard_map(
        local, mesh=mesh, in_specs=placed, out_specs=P("cuts", None, None, "tile"), check_vma=False
    )
```

```python
import functools
import math

import jax
import jax.numpy as jnp
import numpy as np
from jax import lax
from jax.experimental import pallas as pl
from jax.experimental.pallas import tpu as pltpu
from jax.sharding import PartitionSpec as P

F32 = jnp.float32
BF16 = jnp.bfloat16
CORES = 2
ENTRY_SCALE = 1.62475

VMEM = pl.BlockSpec(memory_space=pltpu.VMEM)
SMEM = pl.BlockSpec(memory_space=pltpu.SMEM)
SMALL = pltpu.CompilerParams(vmem_limit_bytes=8 * 2**20)
LARGE = pltpu.CompilerParams(vmem_limit_bytes=24 * 2**20)


def passed_along(block, axis, distance):
    devices = range(lax.axis_size(axis))
    route = [(i - distance, i) for i in devices if i - distance in devices]
    return lax.ppermute(block, axis, route)


def crossed(block, distance):
    size = lax.axis_size("cuts")
    return lax.ppermute(block, "cuts", [(i, i ^ (CORES * distance)) for i in range(size)])


def swapped(block):
    size = lax.axis_size("cuts")
    return lax.ppermute(block, "cuts", [(i, i ^ 1) for i in range(size)])


def dft_blocks(win):
    numbers = np.arange(win)
    angles = (numbers[:, None] * numbers[None, :] % win) * (2.0 * math.pi / win)
    cosine, sine = np.cos(angles) * ENTRY_SCALE, np.sin(angles) * ENTRY_SCALE
    return np.block([[cosine, sine], [-sine, cosine]]).astype(np.float32)


def merge_kernel(chips, slots, win, ints_ref, rows_ref, cols_ref, own_ref, beside_ref, *out_refs):
    row_ids = lax.broadcasted_iota(jnp.int32, (win, win), 0)
    col_ids = lax.broadcasted_iota(jnp.int32, (win, win), 1)
    last = own_ref.shape[1] // win - 1
    for p in range(chips):
        slot = (ints_ref[0] ^ p) // (chips // slots)
        row_at, col_at = rows_ref[slot], cols_ref[slot]
        block = row_at // win
        after = jnp.minimum(block + 1, last)
        upper = row_ids >= row_at - block * win
        mine = col_ids >= col_at
        for part in range(2):
            at = pl.ds(pl.multiple_of(block * win, win), win)
            first = jnp.where(mine, own_ref[part, at, :].astype(F32), beside_ref[part, at, :].astype(F32))
            at = pl.ds(pl.multiple_of(after * win, win), win)
            second = jnp.where(mine, own_ref[part, at, :].astype(F32), beside_ref[part, at, :].astype(F32))
            out_refs[p][part] = jnp.where(upper, first, second).astype(BF16)


def rolled_probe_kernel(win, place_ref, probe_ref, out_ref):
    row_at, col_at = lax.rem(place_ref[0], win), place_ref[1]
    for mode in range(probe_ref.shape[0]):
        for part in range(2):
            block = pltpu.roll(probe_ref[mode, part], row_at, 0)
            out_ref[mode, part] = pltpu.roll(block, col_at, 1).astype(BF16)


def window_kernel(chips, modes, win, *refs):
    slices = CORES * chips
    (ints_ref, weight_ref, left_ref, right_ref, probe_ref, hcos_ref, hsin_ref, target_ref) = refs[:8]
    own_refs = refs[8 : 8 + chips]
    other_refs = refs[8 + chips : 8 + 2 * chips]
    out_refs = refs[8 + 2 * chips : 8 + 3 * chips]
    patch_ref, wave_ref, grad_ref = refs[8 + 3 * chips :]
    chip, core = ints_ref[0], ints_ref[1]
    unit = 1.0 / (ENTRY_SCALE * ENTRY_SCALE * win)
    for p in range(chips):
        source = chip ^ p
        patch_ref[CORES * source + core] = own_refs[p][...]
        patch_ref[CORES * source + 1 - core] = other_refs[p][...]

    def from_left(matrix, pairs):
        stacked = jnp.concatenate(
            [jnp.concatenate([pair[k].astype(BF16) for pair in pairs], 1) for k in range(2)], 0
        )
        prod = jnp.dot(matrix, stacked, preferred_element_type=F32)
        return [
            (prod[:win, m * win : (m + 1) * win], prod[win:, m * win : (m + 1) * win])
            for m in range(modes)
        ]

    def from_right(pairs, matrix):
        stacked = jnp.concatenate(
            [jnp.concatenate([pair[k].astype(BF16) for k in range(2)], 1) for pair in pairs], 0
        )
        prod = jnp.dot(stacked, matrix, preferred_element_type=F32)
        return [
            (prod[m * win : (m + 1) * win, :win], prod[m * win : (m + 1) * win, win:])
            for m in range(modes)
        ]

    def transform(pairs):
        return from_right(from_left(left_ref[...], pairs), right_ref[...])

    def inverse(pairs):
        return from_right(from_left(right_ref[...], pairs), left_ref[...])

    def mul(a, b):
        return (a[0] * b[0] - a[1] * b[1], a[0] * b[1] + a[1] * b[0])

    def conj_mul(a, b):
        return (a[0] * b[0] + a[1] * b[1], a[0] * b[1] - a[1] * b[0])

    def patch_at(s):
        return (patch_ref[s, 0].astype(F32), patch_ref[s, 1].astype(F32))

    def waves_at(s):
        return [(wave_ref[s, m, 0], wave_ref[s, m, 1]) for m in range(modes)]

    def propagator():
        return (hcos_ref[...], hsin_ref[...])

    for m in range(modes):
        for part in range(2):
            wave_ref[0, m, part] = probe_ref[m, part].astype(F32)

    def forward_step(s, carry):
        patch = patch_at(s)
        freq = transform([mul(wave, patch) for wave in waves_at(s)])
        spread = propagator()
        waves = inverse([mul(spread, pair) for pair in freq])
        for m in range(modes):
            for part in range(2):
                wave_ref[s + 1, m, part] = waves[m][part]
        return carry

    lax.fori_loop(0, slices - 1, forward_step, 0)
    patch = patch_at(slices - 1)
    exits = transform([mul(wave, patch) for wave in waves_at(slices - 1)])
    power = sum(pair[0] * pair[0] + pair[1] * pair[1] for pair in exits) * (unit * unit)
    factor = (power - target_ref[...]) * (weight_ref[0] * (0.25 * unit * unit))
    back = inverse([(factor * pair[0], factor * pair[1]) for pair in exits])

    def keep_grad(s, back):
        grads = [conj_mul(wave, pair) for wave, pair in zip(waves_at(s), back)]
        for part in range(2):
            grad_ref[s, part] = sum(grad[part] for grad in grads).astype(BF16)

    keep_grad(slices - 1, back)

    def backward_step(i, back):
        s = slices - 1 - i
        patch = patch_at(s)
        freq = transform([conj_mul(patch, pair) for pair in back])
        spread = propagator()
        back = inverse([conj_mul(spread, pair) for pair in freq])
        keep_grad(s - 1, back)
        return back

    lax.fori_loop(0, slices - 1, backward_step, back)
    for p in range(chips):
        out_refs[p][...] = grad_ref[CORES * (chip ^ p) + core]


def place_kernel(chips, slots, win, groups, from_left, *refs):
    chip_ref, rows_ref, cols_ref = refs[:3]
    block_refs = refs[3 : 3 + len(groups)]
    out_ref = refs[-1]
    if from_left:
        out_ref[...] = refs[3 + len(groups)][...]
    else:
        out_ref[...] = jnp.zeros_like(out_ref)
    row_ids = lax.broadcasted_iota(jnp.int32, (win, win), 0)
    col_ids = lax.broadcasted_iota(jnp.int32, (win, win), 1)
    last = out_ref.shape[1] // win - 1
    copies = chips // slots
    for block_ref, group in zip(block_refs, groups):
        for place, p in enumerate(group):
            source = chip_ref[0] ^ p
            slot = source // copies
            row_at, col_at = rows_ref[slot], cols_ref[slot]
            mine = (col_ids < col_at) if from_left else (col_ids >= col_at)
            counted = lax.rem(source, copies) == 0
            block = row_at // win
            after = jnp.minimum(block + 1, last)
            upper = row_ids >= row_at - block * win
            for part in range(2):
                grad = jnp.where(mine & counted, block_ref[2 * place + part].astype(F32), 0.0)
                at = pl.ds(pl.multiple_of(block * win, win), win)
                out_ref[part, at, :] = out_ref[part, at, :] + jnp.where(upper, grad, 0.0)
                at = pl.ds(pl.multiple_of(after * win, win), win)
                out_ref[part, at, :] = out_ref[part, at, :] + jnp.where(upper, 0.0, grad)


def local(object_slices, probe_modes, prop_phase, measured, row_offsets, col_offsets, counts):
    modes, _, win, _ = probe_modes.shape
    slots = row_offsets.shape[0]
    chips = lax.axis_size("cuts") // CORES
    copies = chips // slots
    assert chips % slots == 0 and chips & (chips - 1) == 0
    section = lax.axis_index("cuts")
    chip, core = section // CORES, section % CORES
    strip = object_slices[0]
    block = jax.ShapeDtypeStruct((2, win, win), BF16)
    order = sorted(range(1, chips), reverse=True)

    own_strip = strip.astype(BF16)
    beside = passed_along(own_strip, "tile", -1)
    ints = jnp.stack([chip, core]).astype(jnp.int32)
    slot = chip // copies
    place = jnp.stack([row_offsets[slot], col_offsets[slot]])
    probe = pl.pallas_call(
        functools.partial(rolled_probe_kernel, win),
        out_shape=jax.ShapeDtypeStruct(probe_modes.shape, BF16),
        in_specs=[SMEM, VMEM],
        out_specs=VMEM,
        compiler_params=SMALL,
    )(place, probe_modes)
    matrix = dft_blocks(win)
    left_matrix = jnp.asarray(matrix, BF16)
    right_matrix = jnp.asarray(matrix.T, BF16)
    unit = 1.0 / (ENTRY_SCALE * ENTRY_SCALE * win)
    hcos = jnp.cos(prop_phase) * (unit * unit)
    hsin = jnp.sin(prop_phase) * (unit * unit)
    target = lax.dynamic_index_in_dim(measured, slot, 0, keepdims=False)
    weight = (slot < counts).astype(F32)

    places = jnp.concatenate([row_offsets, col_offsets])
    probe, hcos, hsin, target, weight, places = lax.optimization_barrier(
        (probe, hcos, hsin, target, weight, places)
    )
    left_places = passed_along(places, "tile", 1)
    beside, left_places = lax.optimization_barrier((beside, left_places))
    left_rows, left_cols = left_places[:slots], left_places[slots:]
    merged = pl.pallas_call(
        functools.partial(merge_kernel, chips, slots, win),
        out_shape=[block] * chips,
        in_specs=[SMEM, SMEM, SMEM, VMEM, VMEM],
        out_specs=[VMEM] * chips,
        compiler_params=SMALL,
    )(ints, row_offsets, col_offsets, own_strip, beside)
    own_blocks = [merged[0]] + [None] * (chips - 1)
    for p in order:
        own_blocks[p] = crossed(merged[p], p)
    other_blocks = [swapped(own_block) for own_block in own_blocks]

    grads = pl.pallas_call(
        functools.partial(window_kernel, chips, modes, win),
        out_shape=[block] * chips,
        in_specs=[SMEM, SMEM] + [VMEM] * (6 + 2 * chips),
        out_specs=[VMEM] * chips,
        scratch_shapes=[
            pltpu.VMEM((CORES * chips, 2, win, win), BF16),
            pltpu.VMEM((CORES * chips, modes, 2, win, win), F32),
            pltpu.VMEM((CORES * chips, 2, win, win), BF16),
        ],
        compiler_params=LARGE,
    )(ints, weight, left_matrix, right_matrix, probe, hcos, hsin, target, *own_blocks, *other_blocks)

    mine = [grads[0]] + [None] * (chips - 1)
    for p in order:
        mine[p] = crossed(grads[p], p)
    early, late = order[: (chips + 1) // 2], order[(chips + 1) // 2 :]
    groups = [[0], early, late]
    wrapped = [
        passed_along(jnp.concatenate([mine[p] for p in group], 0), "tile", 1) for group in groups
    ]

    def placed(groups, from_left, rows, cols, *arrays):
        return pl.pallas_call(
            functools.partial(place_kernel, chips, slots, win, groups, from_left),
            out_shape=jax.ShapeDtypeStruct(strip.shape, F32),
            in_specs=[SMEM, SMEM, SMEM] + [VMEM] * len(arrays),
            out_specs=VMEM,
            input_output_aliases={3 + len(groups): 0} if from_left else {},
            compiler_params=SMALL,
        )(ints, rows, cols, *arrays)

    own_part = placed([[p] for p in range(chips)], False, row_offsets, col_offsets, *mine)
    return placed(groups, True, left_rows, left_cols, *wrapped, own_part)[None]


def solution(mesh):
    placed = (
        P("cuts", None, None, "tile"),
        P(),
        P(),
        P("tile", None, None),
        P("tile"),
        P("tile"),
        P("tile"),
    )
    return jax.shard_map(
        local, mesh=mesh, in_specs=placed, out_specs=P("cuts", None, None, "tile"), check_vma=False
    )
```

```python
import functools
import math

import jax
import jax.numpy as jnp
import numpy as np
from jax import lax
from jax.experimental import pallas as pl
from jax.experimental.pallas import tpu as pltpu
from jax.sharding import PartitionSpec as P

F32 = jnp.float32
BF16 = jnp.bfloat16
CORES = 2
ENTRY_SCALE = 1.62475

VMEM = pl.BlockSpec(memory_space=pltpu.VMEM)
SMEM = pl.BlockSpec(memory_space=pltpu.SMEM)
SMALL = pltpu.CompilerParams(vmem_limit_bytes=8 * 2**20)
LARGE = pltpu.CompilerParams(vmem_limit_bytes=24 * 2**20)


def passed_round(block, axis, distance):
    size = lax.axis_size(axis)
    return lax.ppermute(block, axis, [(i, (i + distance) % size) for i in range(size)])


def crossed(block, distance):
    size = lax.axis_size("cuts")
    return lax.ppermute(block, "cuts", [(i, i ^ (CORES * distance)) for i in range(size)])


def swapped(block):
    size = lax.axis_size("cuts")
    return lax.ppermute(block, "cuts", [(i, i ^ 1) for i in range(size)])


def dft_blocks(win):
    numbers = np.arange(win)
    angles = (numbers[:, None] * numbers[None, :] % win) * (2.0 * math.pi / win)
    cosine, sine = np.cos(angles) * ENTRY_SCALE, np.sin(angles) * ENTRY_SCALE
    return np.block([[cosine, sine], [-sine, cosine]]).astype(np.float32)


def merge_kernel(chips, slots, win, ints_ref, rows_ref, cols_ref, own_ref, beside_ref, *out_refs):
    row_ids = lax.broadcasted_iota(jnp.int32, (win, win), 0)
    col_ids = lax.broadcasted_iota(jnp.int32, (win, win), 1)
    last = own_ref.shape[1] // win - 1
    inside = ints_ref[2] == 0

    def columns(part, at, mine):
        beside = jnp.where(inside, beside_ref[part, at, :].astype(F32), 0.0)
        return jnp.where(mine, own_ref[part, at, :].astype(F32), beside)

    for p in range(chips):
        slot = (ints_ref[0] ^ p) // (chips // slots)
        row_at, col_at = rows_ref[slot], cols_ref[slot]
        block = row_at // win
        after = jnp.minimum(block + 1, last)
        upper = row_ids >= row_at - block * win
        mine = col_ids >= col_at
        for part in range(2):
            at = pl.ds(pl.multiple_of(block * win, win), win)
            first = columns(part, at, mine)
            at = pl.ds(pl.multiple_of(after * win, win), win)
            second = columns(part, at, mine)
            out_refs[p][part] = jnp.where(upper, first, second).astype(BF16)


def rolled_probe_kernel(win, place_ref, probe_ref, out_ref):
    row_at, col_at = lax.rem(place_ref[0], win), place_ref[1]
    for mode in range(probe_ref.shape[0]):
        for part in range(2):
            block = pltpu.roll(probe_ref[mode, part], row_at, 0)
            out_ref[mode, part] = pltpu.roll(block, col_at, 1).astype(BF16)


def window_kernel(chips, modes, win, groups, *refs):
    slices = CORES * chips
    (ints_ref, weight_ref, left_ref, right_ref, probe_ref, hcos_ref, hsin_ref, target_ref) = refs[:8]
    own_refs = refs[8 : 8 + chips]
    refs = refs[8 + chips :]
    other_refs, refs = refs[: len(groups)], refs[len(groups) :]
    out_refs, (patch_ref, wave_ref, grad_ref) = refs[:chips], refs[chips:]
    chip, core = ints_ref[0], ints_ref[1]
    unit = 1.0 / (ENTRY_SCALE * ENTRY_SCALE * win)
    for p in range(chips):
        patch_ref[CORES * (chip ^ p) + core] = own_refs[p][...]
    for other_ref, group in zip(other_refs, groups):
        for place, p in enumerate(group):
            patch_ref[CORES * (chip ^ p) + 1 - core] = other_ref[2 * place : 2 * place + 2]

    def from_left(matrix, pairs):
        stacked = jnp.concatenate(
            [jnp.concatenate([pair[k].astype(BF16) for pair in pairs], 1) for k in range(2)], 0
        )
        prod = jnp.dot(matrix, stacked, preferred_element_type=F32)
        return [
            (prod[:win, m * win : (m + 1) * win], prod[win:, m * win : (m + 1) * win])
            for m in range(modes)
        ]

    def from_right(pairs, matrix):
        stacked = jnp.concatenate(
            [jnp.concatenate([pair[k].astype(BF16) for k in range(2)], 1) for pair in pairs], 0
        )
        prod = jnp.dot(stacked, matrix, preferred_element_type=F32)
        return [
            (prod[m * win : (m + 1) * win, :win], prod[m * win : (m + 1) * win, win:])
            for m in range(modes)
        ]

    def transform(pairs):
        return from_right(from_left(left_ref[...], pairs), right_ref[...])

    def inverse(pairs):
        return from_right(from_left(right_ref[...], pairs), left_ref[...])

    def mul(a, b):
        return (a[0] * b[0] - a[1] * b[1], a[0] * b[1] + a[1] * b[0])

    def conj_mul(a, b):
        return (a[0] * b[0] + a[1] * b[1], a[0] * b[1] - a[1] * b[0])

    def patch_at(s):
        return (patch_ref[s, 0].astype(F32), patch_ref[s, 1].astype(F32))

    def waves_at(s):
        return [(wave_ref[s, m, 0], wave_ref[s, m, 1]) for m in range(modes)]

    def propagator():
        return (hcos_ref[...], hsin_ref[...])

    for m in range(modes):
        for part in range(2):
            wave_ref[0, m, part] = probe_ref[m, part].astype(F32)

    def forward_step(s, carry):
        patch = patch_at(s)
        freq = transform([mul(wave, patch) for wave in waves_at(s)])
        spread = propagator()
        waves = inverse([mul(spread, pair) for pair in freq])
        for m in range(modes):
            for part in range(2):
                wave_ref[s + 1, m, part] = waves[m][part]
        return carry

    lax.fori_loop(0, slices - 1, forward_step, 0)
    patch = patch_at(slices - 1)
    exits = transform([mul(wave, patch) for wave in waves_at(slices - 1)])
    power = sum(pair[0] * pair[0] + pair[1] * pair[1] for pair in exits) * (unit * unit)
    factor = (power - target_ref[...]) * (weight_ref[0] * (0.25 * unit * unit))
    back = inverse([(factor * pair[0], factor * pair[1]) for pair in exits])

    def keep_grad(s, back):
        grads = [conj_mul(wave, pair) for wave, pair in zip(waves_at(s), back)]
        for part in range(2):
            grad_ref[s, part] = sum(grad[part] for grad in grads).astype(BF16)

    keep_grad(slices - 1, back)

    def backward_step(i, back):
        s = slices - 1 - i
        patch = patch_at(s)
        freq = transform([conj_mul(patch, pair) for pair in back])
        spread = propagator()
        back = inverse([conj_mul(spread, pair) for pair in freq])
        keep_grad(s - 1, back)
        return back

    lax.fori_loop(0, slices - 1, backward_step, back)
    for p in range(chips):
        out_refs[p][...] = grad_ref[CORES * (chip ^ p) + core]


def place_kernel(chips, slots, win, groups, from_left, *refs):
    chip_ref, rows_ref, cols_ref = refs[:3]
    block_refs = refs[3 : 3 + len(groups)]
    out_ref = refs[-1]
    part = pl.program_id(0)
    if from_left:
        out_ref[0] = refs[3 + len(groups)][part]
    else:
        out_ref[...] = jnp.zeros_like(out_ref)
    row_ids = lax.broadcasted_iota(jnp.int32, (win, win), 0)
    col_ids = lax.broadcasted_iota(jnp.int32, (win, win), 1)
    last = out_ref.shape[1] // win - 1
    copies = chips // slots
    for block_ref, group in zip(block_refs, groups):
        for place, p in enumerate(group):
            source = chip_ref[0] ^ p
            slot = source // copies
            row_at, col_at = rows_ref[slot], cols_ref[slot]
            mine = (col_ids < col_at) if from_left else (col_ids >= col_at)
            counted = lax.rem(source, copies) == 0
            block = row_at // win
            after = jnp.minimum(block + 1, last)
            upper = row_ids >= row_at - block * win
            grad = jnp.where(mine & counted, block_ref[2 * place + part].astype(F32), 0.0)
            at = pl.ds(pl.multiple_of(block * win, win), win)
            out_ref[0, at, :] = out_ref[0, at, :] + jnp.where(upper, grad, 0.0)
            at = pl.ds(pl.multiple_of(after * win, win), win)
            out_ref[0, at, :] = out_ref[0, at, :] + jnp.where(upper, 0.0, grad)


def local(object_slices, probe_modes, prop_phase, measured, row_offsets, col_offsets, counts):
    modes, _, win, _ = probe_modes.shape
    slots = row_offsets.shape[0]
    chips = lax.axis_size("cuts") // CORES
    copies = chips // slots
    assert chips % slots == 0 and chips & (chips - 1) == 0
    section = lax.axis_index("cuts")
    chip, core = section // CORES, section % CORES
    strip = object_slices[0]
    block = jax.ShapeDtypeStruct((2, win, win), BF16)
    order = sorted(range(1, chips), reverse=True)
    near, far = list(range(chips // 2)), [p for p in order if p >= chips // 2]

    def joined(blocks, group):
        return jnp.concatenate([blocks[p] for p in group], 0) if len(group) > 1 else blocks[group[0]]


    own_strip = strip.astype(BF16)
    beside = passed_round(own_strip, "tile", -1)
    tile = lax.axis_index("tile")
    rightmost = tile == lax.axis_size("tile") - 1
    ints = jnp.stack([chip, core, rightmost]).astype(jnp.int32)
    slot = chip // copies
    place = jnp.stack([row_offsets[slot], col_offsets[slot]])
    probe = pl.pallas_call(
        functools.partial(rolled_probe_kernel, win),
        out_shape=jax.ShapeDtypeStruct(probe_modes.shape, BF16),
        in_specs=[SMEM, VMEM],
        out_specs=VMEM,
        compiler_params=SMALL,
    )(place, probe_modes)
    matrix = dft_blocks(win)
    left_matrix = jnp.asarray(matrix, BF16)
    right_matrix = jnp.asarray(matrix.T, BF16)
    unit = 1.0 / (ENTRY_SCALE * ENTRY_SCALE * win)
    hcos = jnp.cos(prop_phase) * (unit * unit)
    hsin = jnp.sin(prop_phase) * (unit * unit)
    target = lax.dynamic_index_in_dim(measured, slot, 0, keepdims=False)
    weight = (slot < counts).astype(F32)

    note = jnp.stack([row_offsets // win, row_offsets % win, col_offsets]).astype(BF16)
    note = jnp.pad(note, ((0, 16 - 3), (0, win - slots)))
    beside, probe, hcos, hsin, target, weight, note = lax.optimization_barrier(
        (beside, probe, hcos, hsin, target, weight, note)
    )
    merged = pl.pallas_call(
        functools.partial(merge_kernel, chips, slots, win),
        out_shape=[block] * chips,
        in_specs=[SMEM, SMEM, SMEM, VMEM, VMEM],
        out_specs=[VMEM] * chips,
        compiler_params=SMALL,
    )(ints, row_offsets, col_offsets, own_strip, beside)
    own_blocks = [merged[0]] + [None] * (chips - 1)
    for p in order:
        own_blocks[p] = crossed(merged[p], p)
    swaps = [near] + [[p] for p in far]
    other_blocks = [swapped(joined(own_blocks, group)) for group in swaps]

    grads = pl.pallas_call(
        functools.partial(window_kernel, chips, modes, win, swaps),
        out_shape=[block] * chips,
        in_specs=[SMEM, SMEM] + [VMEM] * (6 + chips + len(swaps)),
        out_specs=[VMEM] * chips,
        scratch_shapes=[
            pltpu.VMEM((CORES * chips, 2, win, win), BF16),
            pltpu.VMEM((CORES * chips, modes, 2, win, win), F32),
            pltpu.VMEM((CORES * chips, 2, win, win), BF16),
        ],
        compiler_params=LARGE,
    )(ints, weight, left_matrix, right_matrix, probe, hcos, hsin, target, *own_blocks, *other_blocks)

    mine = [grads[0]] + [None] * (chips - 1)
    for p in order:
        mine[p] = crossed(grads[p], p)
    size = len(near) * 2 * win
    first = jnp.concatenate([mine[p].reshape(2 * win, win) for p in near] + [note], 0)
    first = passed_round(first, "tile", 1)
    places = first[size : size + 3, :slots].astype(jnp.int32)
    left_rows, left_cols = places[0] * win + places[1], jnp.where(tile > 0, places[2], 0)
    groups = [near, far]
    wrapped = [first[:size].reshape(-1, win, win), passed_round(joined(mine, far), "tile", 1)]

    def placed(groups, from_left, rows, cols, *arrays):
        return pl.pallas_call(
            functools.partial(place_kernel, chips, slots, win, groups, from_left),
            out_shape=jax.ShapeDtypeStruct(strip.shape, F32),
            grid=(2,),
            in_specs=[SMEM, SMEM, SMEM] + [VMEM] * len(arrays),
            out_specs=pl.BlockSpec((1,) + strip.shape[1:], lambda part: (part, 0, 0)),
            compiler_params=SMALL,
        )(ints, rows, cols, *arrays)

    own_part = placed([[p] for p in range(chips)], False, row_offsets, col_offsets, *mine)
    return placed(groups, True, left_rows, left_cols, *wrapped, own_part)[None]


def solution(mesh):
    placed = (
        P("cuts", None, None, "tile"),
        P(),
        P(),
        P("tile", None, None),
        P("tile"),
        P("tile"),
        P("tile"),
    )
    return jax.shard_map(
        local, mesh=mesh, in_specs=placed, out_specs=P("cuts", None, None, "tile"), check_vma=False
    )
```

```python
import functools
import math

import jax
import jax.numpy as jnp
import numpy as np
from jax import lax
from jax.experimental import pallas as pl
from jax.experimental.pallas import tpu as pltpu
from jax.sharding import PartitionSpec as P

F32 = jnp.float32
BF16 = jnp.bfloat16
CORES = 2
ENTRY_SCALE = 1.62475

VMEM = pl.BlockSpec(memory_space=pltpu.VMEM)
SMEM = pl.BlockSpec(memory_space=pltpu.SMEM)
SMALL = pltpu.CompilerParams(vmem_limit_bytes=8 * 2**20)
LARGE = pltpu.CompilerParams(vmem_limit_bytes=24 * 2**20)


def passed_round(block, axis, distance):
    size = lax.axis_size(axis)
    return lax.ppermute(block, axis, [(i, (i + distance) % size) for i in range(size)])


def crossed(block, distance):
    size = lax.axis_size("cuts")
    return lax.ppermute(block, "cuts", [(i, i ^ (CORES * distance)) for i in range(size)])


def swapped(block):
    size = lax.axis_size("cuts")
    return lax.ppermute(block, "cuts", [(i, i ^ 1) for i in range(size)])


def dft_blocks(win):
    numbers = np.arange(win)
    angles = (numbers[:, None] * numbers[None, :] % win) * (2.0 * math.pi / win)
    cosine, sine = np.cos(angles) * ENTRY_SCALE, np.sin(angles) * ENTRY_SCALE
    return np.block([[cosine, sine], [-sine, cosine]]).astype(np.float32)


def merge_kernel(chips, slots, win, ints_ref, rows_ref, cols_ref, own_ref, beside_ref, *out_refs):
    row_ids = lax.broadcasted_iota(jnp.int32, (win, win), 0)
    col_ids = lax.broadcasted_iota(jnp.int32, (win, win), 1)
    last = own_ref.shape[1] // win - 1
    inside = ints_ref[2] == 0

    def columns(part, at, mine):
        beside = jnp.where(inside, beside_ref[part, at, :].astype(F32), 0.0)
        return jnp.where(mine, own_ref[part, at, :].astype(F32), beside)

    for p in range(chips):
        slot = (ints_ref[0] ^ p) // (chips // slots)
        row_at, col_at = rows_ref[slot], cols_ref[slot]
        block = row_at // win
        after = jnp.minimum(block + 1, last)
        upper = row_ids >= row_at - block * win
        mine = col_ids >= col_at
        for part in range(2):
            at = pl.ds(pl.multiple_of(block * win, win), win)
            first = columns(part, at, mine)
            at = pl.ds(pl.multiple_of(after * win, win), win)
            second = columns(part, at, mine)
            out_refs[p][part] = jnp.where(upper, first, second).astype(BF16)


def rolled_probe_kernel(win, place_ref, probe_ref, out_ref):
    row_at, col_at = lax.rem(place_ref[0], win), place_ref[1]
    for mode in range(probe_ref.shape[0]):
        for part in range(2):
            block = pltpu.roll(probe_ref[mode, part], row_at, 0)
            out_ref[mode, part] = pltpu.roll(block, col_at, 1).astype(BF16)


def window_kernel(chips, modes, win, groups, *refs):
    slices = CORES * chips
    (ints_ref, weight_ref, left_ref, right_ref, probe_ref, hcos_ref, hsin_ref, target_ref) = refs[:8]
    own_refs = refs[8 : 8 + chips]
    refs = refs[8 + chips :]
    other_refs, refs = refs[: len(groups)], refs[len(groups) :]
    out_refs, (patch_ref, wave_ref, grad_ref) = refs[:chips], refs[chips:]
    chip, core = ints_ref[0], ints_ref[1]
    unit = 1.0 / (ENTRY_SCALE * ENTRY_SCALE * win)
    for p in range(chips):
        patch_ref[CORES * (chip ^ p) + core] = own_refs[p][...]
    for other_ref, group in zip(other_refs, groups):
        for place, p in enumerate(group):
            patch_ref[CORES * (chip ^ p) + 1 - core] = other_ref[2 * place : 2 * place + 2]

    def from_left(matrix, pairs):
        stacked = jnp.concatenate(
            [jnp.concatenate([pair[k].astype(BF16) for pair in pairs], 1) for k in range(2)], 0
        )
        prod = jnp.dot(matrix, stacked, preferred_element_type=F32)
        return [
            (prod[:win, m * win : (m + 1) * win], prod[win:, m * win : (m + 1) * win])
            for m in range(modes)
        ]

    def from_right(pairs, matrix):
        stacked = jnp.concatenate(
            [jnp.concatenate([pair[k].astype(BF16) for k in range(2)], 1) for pair in pairs], 0
        )
        prod = jnp.dot(stacked, matrix, preferred_element_type=F32)
        return [
            (prod[m * win : (m + 1) * win, :win], prod[m * win : (m + 1) * win, win:])
            for m in range(modes)
        ]

    def transform(pairs):
        return from_right(from_left(left_ref[...], pairs), right_ref[...])

    def inverse(pairs):
        return from_left(right_ref[...], from_right(pairs, left_ref[...]))

    def mul(a, b):
        return (a[0] * b[0] - a[1] * b[1], a[0] * b[1] + a[1] * b[0])

    def conj_mul(a, b):
        return (a[0] * b[0] + a[1] * b[1], a[0] * b[1] - a[1] * b[0])

    def patch_at(s):
        return (patch_ref[s, 0].astype(F32), patch_ref[s, 1].astype(F32))

    def waves_at(s):
        return [(wave_ref[s, m, 0], wave_ref[s, m, 1]) for m in range(modes)]

    def propagator():
        return (hcos_ref[...], hsin_ref[...])

    for m in range(modes):
        for part in range(2):
            wave_ref[0, m, part] = probe_ref[m, part].astype(F32)

    def forward_step(s, carry):
        patch = patch_at(s)
        freq = transform([mul(wave, patch) for wave in waves_at(s)])
        spread = propagator()
        waves = inverse([mul(spread, pair) for pair in freq])
        for m in range(modes):
            for part in range(2):
                wave_ref[s + 1, m, part] = waves[m][part]
        return carry

    lax.fori_loop(0, slices - 1, forward_step, 0, unroll=True)
    patch = patch_at(slices - 1)
    exits = transform([mul(wave, patch) for wave in waves_at(slices - 1)])
    power = sum(pair[0] * pair[0] + pair[1] * pair[1] for pair in exits) * (unit * unit)
    factor = (power - target_ref[...]) * (weight_ref[0] * (0.25 * unit * unit))
    back = inverse([(factor * pair[0], factor * pair[1]) for pair in exits])

    def keep_grad(s, back):
        grads = [conj_mul(wave, pair) for wave, pair in zip(waves_at(s), back)]
        for part in range(2):
            grad_ref[s, part] = sum(grad[part] for grad in grads).astype(BF16)

    keep_grad(slices - 1, back)

    def backward_step(i, back):
        s = slices - 1 - i
        patch = patch_at(s)
        freq = transform([conj_mul(patch, pair) for pair in back])
        spread = propagator()
        back = inverse([conj_mul(spread, pair) for pair in freq])
        keep_grad(s - 1, back)
        return back

    lax.fori_loop(0, slices - 1, backward_step, back, unroll=True)
    for p in range(chips):
        out_refs[p][...] = grad_ref[CORES * (chip ^ p) + core]


def place_kernel(chips, slots, win, groups, from_left, *refs):
    chip_ref, rows_ref, cols_ref = refs[:3]
    block_refs = refs[3 : 3 + len(groups)]
    out_ref = refs[-1]
    part = pl.program_id(0)
    if from_left:
        out_ref[0] = refs[3 + len(groups)][part]
    else:
        out_ref[...] = jnp.zeros_like(out_ref)
    row_ids = lax.broadcasted_iota(jnp.int32, (win, win), 0)
    col_ids = lax.broadcasted_iota(jnp.int32, (win, win), 1)
    last = out_ref.shape[1] // win - 1
    copies = chips // slots
    for block_ref, group in zip(block_refs, groups):
        for place, p in enumerate(group):
            source = chip_ref[0] ^ p
            slot = source // copies
            row_at, col_at = rows_ref[slot], cols_ref[slot]
            mine = (col_ids < col_at) if from_left else (col_ids >= col_at)
            counted = lax.rem(source, copies) == 0
            block = row_at // win
            after = jnp.minimum(block + 1, last)
            upper = row_ids >= row_at - block * win
            grad = jnp.where(mine & counted, block_ref[2 * place + part].astype(F32), 0.0)
            at = pl.ds(pl.multiple_of(block * win, win), win)
            out_ref[0, at, :] = out_ref[0, at, :] + jnp.where(upper, grad, 0.0)
            at = pl.ds(pl.multiple_of(after * win, win), win)
            out_ref[0, at, :] = out_ref[0, at, :] + jnp.where(upper, 0.0, grad)


def local(object_slices, probe_modes, prop_phase, measured, row_offsets, col_offsets, counts):
    modes, _, win, _ = probe_modes.shape
    slots = row_offsets.shape[0]
    chips = lax.axis_size("cuts") // CORES
    copies = chips // slots
    assert chips % slots == 0 and chips & (chips - 1) == 0
    section = lax.axis_index("cuts")
    chip, core = section // CORES, section % CORES
    strip = object_slices[0]
    block = jax.ShapeDtypeStruct((2, win, win), BF16)
    order = sorted(range(1, chips), reverse=True)
    near, far = list(range(chips // 2)), [p for p in order if p >= chips // 2]

    def joined(blocks, group):
        return jnp.concatenate([blocks[p] for p in group], 0) if len(group) > 1 else blocks[group[0]]


    own_strip = strip.astype(BF16)
    beside = passed_round(own_strip, "tile", -1)
    tile = lax.axis_index("tile")
    rightmost = tile == lax.axis_size("tile") - 1
    ints = jnp.stack([chip, core, rightmost]).astype(jnp.int32)
    slot = chip // copies
    place = jnp.stack([row_offsets[slot], col_offsets[slot]])
    probe = pl.pallas_call(
        functools.partial(rolled_probe_kernel, win),
        out_shape=jax.ShapeDtypeStruct(probe_modes.shape, BF16),
        in_specs=[SMEM, VMEM],
        out_specs=VMEM,
        compiler_params=SMALL,
    )(place, probe_modes)
    matrix = dft_blocks(win)
    left_matrix = jnp.asarray(matrix, BF16)
    right_matrix = jnp.asarray(matrix.T, BF16)
    unit = 1.0 / (ENTRY_SCALE * ENTRY_SCALE * win)
    hcos = jnp.cos(prop_phase) * (unit * unit)
    hsin = jnp.sin(prop_phase) * (unit * unit)
    target = lax.dynamic_index_in_dim(measured, slot, 0, keepdims=False)
    weight = (slot < counts).astype(F32)

    note = jnp.stack([row_offsets // win, row_offsets % win, col_offsets]).astype(BF16)
    note = jnp.pad(note, ((0, 16 - 3), (0, win - slots)))
    beside, probe, hcos, hsin, target, weight, note = lax.optimization_barrier(
        (beside, probe, hcos, hsin, target, weight, note)
    )
    merged = pl.pallas_call(
        functools.partial(merge_kernel, chips, slots, win),
        out_shape=[block] * chips,
        in_specs=[SMEM, SMEM, SMEM, VMEM, VMEM],
        out_specs=[VMEM] * chips,
        compiler_params=SMALL,
    )(ints, row_offsets, col_offsets, own_strip, beside)
    own_blocks = [merged[0]] + [None] * (chips - 1)
    for p in order:
        own_blocks[p] = crossed(merged[p], p)
    swaps = [near] + [[p] for p in far]
    other_blocks = [swapped(joined(own_blocks, group)) for group in swaps]

    grads = pl.pallas_call(
        functools.partial(window_kernel, chips, modes, win, swaps),
        out_shape=[block] * chips,
        in_specs=[SMEM, SMEM] + [VMEM] * (6 + chips + len(swaps)),
        out_specs=[VMEM] * chips,
        scratch_shapes=[
            pltpu.VMEM((CORES * chips, 2, win, win), BF16),
            pltpu.VMEM((CORES * chips, modes, 2, win, win), F32),
            pltpu.VMEM((CORES * chips, 2, win, win), BF16),
        ],
        compiler_params=LARGE,
    )(ints, weight, left_matrix, right_matrix, probe, hcos, hsin, target, *own_blocks, *other_blocks)

    mine = [grads[0]] + [None] * (chips - 1)
    for p in order:
        mine[p] = crossed(grads[p], p)
    size = len(near) * 2 * win
    first = jnp.concatenate([mine[p].reshape(2 * win, win) for p in near] + [note], 0)
    first = passed_round(first, "tile", 1)
    places = first[size : size + 3, :slots].astype(jnp.int32)
    left_rows, left_cols = places[0] * win + places[1], jnp.where(tile > 0, places[2], 0)
    groups = [near, far]
    wrapped = [first[:size].reshape(-1, win, win), passed_round(joined(mine, far), "tile", 1)]

    def placed(groups, from_left, rows, cols, *arrays):
        return pl.pallas_call(
            functools.partial(place_kernel, chips, slots, win, groups, from_left),
            out_shape=jax.ShapeDtypeStruct(strip.shape, F32),
            grid=(2,),
            in_specs=[SMEM, SMEM, SMEM] + [VMEM] * len(arrays),
            out_specs=pl.BlockSpec((1,) + strip.shape[1:], lambda part: (part, 0, 0)),
            compiler_params=SMALL,
        )(ints, rows, cols, *arrays)

    own_part = placed([[p] for p in range(chips)], False, row_offsets, col_offsets, *mine)
    return placed(groups, True, left_rows, left_cols, *wrapped, own_part)[None]


def solution(mesh):
    placed = (
        P("cuts", None, None, "tile"),
        P(),
        P(),
        P("tile", None, None),
        P("tile"),
        P("tile"),
        P("tile"),
    )
    return jax.shard_map(
        local, mesh=mesh, in_specs=placed, out_specs=P("cuts", None, None, "tile"), check_vma=False
    )
```

```python
import functools
import math

import jax
import jax.numpy as jnp
import numpy as np
from jax import lax
from jax.experimental import pallas as pl
from jax.experimental.pallas import tpu as pltpu
from jax.sharding import PartitionSpec as P

F32 = jnp.float32
BF16 = jnp.bfloat16
CORES = 2
ENTRY_SCALE = 1.62475

VMEM = pl.BlockSpec(memory_space=pltpu.VMEM)
SMEM = pl.BlockSpec(memory_space=pltpu.SMEM)
SMALL = pltpu.CompilerParams(vmem_limit_bytes=8 * 2**20)
LARGE = pltpu.CompilerParams(vmem_limit_bytes=24 * 2**20)


def passed_round(block, axis, distance):
    size = lax.axis_size(axis)
    return lax.ppermute(block, axis, [(i, (i + distance) % size) for i in range(size)])


def crossed(block, distance):
    size = lax.axis_size("cuts")
    return lax.ppermute(block, "cuts", [(i, i ^ (CORES * distance)) for i in range(size)])


def swapped(block):
    size = lax.axis_size("cuts")
    return lax.ppermute(block, "cuts", [(i, i ^ 1) for i in range(size)])


def dft_blocks(win):
    numbers = np.arange(win)
    angles = (numbers[:, None] * numbers[None, :] % win) * (2.0 * math.pi / win)
    cosine, sine = np.cos(angles) * ENTRY_SCALE, np.sin(angles) * ENTRY_SCALE
    return np.block([[cosine, sine], [-sine, cosine]]).astype(np.float32)


def merge_kernel(chips, slots, win, ints_ref, rows_ref, cols_ref, own_ref, beside_ref, *out_refs):
    row_ids = lax.broadcasted_iota(jnp.int32, (win, win), 0)
    col_ids = lax.broadcasted_iota(jnp.int32, (win, win), 1)
    last = own_ref.shape[1] // win - 1
    inside = ints_ref[2] == 0

    def columns(part, at, mine):
        beside = jnp.where(inside, beside_ref[part, at, :].astype(F32), 0.0)
        return jnp.where(mine, own_ref[part, at, :].astype(F32), beside)

    for p in range(chips):
        slot = (ints_ref[0] ^ p) // (chips // slots)
        row_at, col_at = rows_ref[slot], cols_ref[slot]
        block = row_at // win
        after = jnp.minimum(block + 1, last)
        upper = row_ids >= row_at - block * win
        mine = col_ids >= col_at
        for part in range(2):
            at = pl.ds(pl.multiple_of(block * win, win), win)
            first = columns(part, at, mine)
            at = pl.ds(pl.multiple_of(after * win, win), win)
            second = columns(part, at, mine)
            out_refs[p][part] = jnp.where(upper, first, second).astype(BF16)


def rolled_probe_kernel(win, place_ref, probe_ref, out_ref):
    row_at, col_at = lax.rem(place_ref[0], win), place_ref[1]
    for mode in range(probe_ref.shape[0]):
        for part in range(2):
            block = pltpu.roll(probe_ref[mode, part], row_at, 0)
            out_ref[mode, part] = pltpu.roll(block, col_at, 1).astype(BF16)


def window_kernel(chips, modes, win, groups, *refs):
    slices = CORES * chips
    (ints_ref, weight_ref, left_ref, right_ref, probe_ref, hcos_ref, hsin_ref, target_ref) = refs[:8]
    own_refs = refs[8 : 8 + chips]
    refs = refs[8 + chips :]
    other_refs, refs = refs[: len(groups)], refs[len(groups) :]
    out_refs, (patch_ref, wave_ref, grad_ref) = refs[:chips], refs[chips:]
    chip, core = ints_ref[0], ints_ref[1]
    unit = 1.0 / (ENTRY_SCALE * ENTRY_SCALE * win)
    for p, own_ref in zip(reversed(range(chips)), own_refs):
        patch_ref[CORES * (chip ^ p) + core] = own_ref[...]
    for other_ref, group in zip(other_refs, groups):
        for place, p in enumerate(group):
            patch_ref[CORES * (chip ^ p) + 1 - core] = other_ref[2 * place : 2 * place + 2]

    def from_left(matrix, pairs):
        stacked = jnp.concatenate(
            [jnp.concatenate([pair[k].astype(BF16) for pair in pairs], 1) for k in range(2)], 0
        )
        prod = jnp.dot(matrix, stacked, preferred_element_type=F32)
        return [
            (prod[:win, m * win : (m + 1) * win], prod[win:, m * win : (m + 1) * win])
            for m in range(modes)
        ]

    def from_right(pairs, matrix):
        stacked = jnp.concatenate(
            [jnp.concatenate([pair[k].astype(BF16) for k in range(2)], 1) for pair in pairs], 0
        )
        prod = jnp.dot(stacked, matrix, preferred_element_type=F32)
        return [
            (prod[m * win : (m + 1) * win, :win], prod[m * win : (m + 1) * win, win:])
            for m in range(modes)
        ]

    def transform(pairs):
        return from_right(from_left(left_ref[...], pairs), right_ref[...])

    def inverse(pairs):
        return from_left(right_ref[...], from_right(pairs, left_ref[...]))

    def mul(a, b):
        return (a[0] * b[0] - a[1] * b[1], a[0] * b[1] + a[1] * b[0])

    def conj_mul(a, b):
        return (a[0] * b[0] + a[1] * b[1], a[0] * b[1] - a[1] * b[0])

    def patch_at(s):
        return (patch_ref[s, 0].astype(F32), patch_ref[s, 1].astype(F32))

    def waves_at(s):
        return [(wave_ref[s, m, 0], wave_ref[s, m, 1]) for m in range(modes)]

    def propagator():
        return (hcos_ref[...], hsin_ref[...])

    for m in range(modes):
        for part in range(2):
            wave_ref[0, m, part] = probe_ref[m, part].astype(F32)

    def forward_step(s, carry):
        patch = patch_at(s)
        freq = transform([mul(wave, patch) for wave in waves_at(s)])
        spread = propagator()
        waves = inverse([mul(spread, pair) for pair in freq])
        for m in range(modes):
            for part in range(2):
                wave_ref[s + 1, m, part] = waves[m][part]
        return carry

    lax.fori_loop(0, slices - 1, forward_step, 0, unroll=True)
    patch = patch_at(slices - 1)
    exits = transform([mul(wave, patch) for wave in waves_at(slices - 1)])
    power = sum(pair[0] * pair[0] + pair[1] * pair[1] for pair in exits) * (unit * unit)
    factor = (power - target_ref[...]) * (weight_ref[0] * (0.25 * unit * unit))
    back = inverse([(factor * pair[0], factor * pair[1]) for pair in exits])

    def keep_grad(s, back):
        grads = [conj_mul(wave, pair) for wave, pair in zip(waves_at(s), back)]
        for part in range(2):
            grad_ref[s, part] = sum(grad[part] for grad in grads).astype(BF16)

    keep_grad(slices - 1, back)

    def backward_step(i, back):
        s = slices - 1 - i
        patch = patch_at(s)
        freq = transform([conj_mul(patch, pair) for pair in back])
        spread = propagator()
        back = inverse([conj_mul(spread, pair) for pair in freq])
        keep_grad(s - 1, back)
        return back

    lax.fori_loop(0, slices - 1, backward_step, back, unroll=True)
    for p in range(chips):
        out_refs[p][...] = grad_ref[CORES * (chip ^ p) + core]


def place_kernel(chips, slots, win, groups, from_left, *refs):
    chip_ref, rows_ref, cols_ref = refs[:3]
    block_refs = refs[3 : 3 + len(groups)]
    out_ref = refs[-1]
    part = pl.program_id(0)
    if from_left:
        out_ref[0] = refs[3 + len(groups)][part]
    else:
        out_ref[...] = jnp.zeros_like(out_ref)
    row_ids = lax.broadcasted_iota(jnp.int32, (win, win), 0)
    col_ids = lax.broadcasted_iota(jnp.int32, (win, win), 1)
    last = out_ref.shape[1] // win - 1
    copies = chips // slots
    for block_ref, group in zip(block_refs, groups):
        for place, p in enumerate(group):
            source = chip_ref[0] ^ p
            slot = source // copies
            row_at, col_at = rows_ref[slot], cols_ref[slot]
            mine = (col_ids < col_at) if from_left else (col_ids >= col_at)
            counted = lax.rem(source, copies) == 0
            block = row_at // win
            after = jnp.minimum(block + 1, last)
            upper = row_ids >= row_at - block * win
            grad = jnp.where(mine & counted, block_ref[2 * place + part].astype(F32), 0.0)
            at = pl.ds(pl.multiple_of(block * win, win), win)
            out_ref[0, at, :] = out_ref[0, at, :] + jnp.where(upper, grad, 0.0)
            at = pl.ds(pl.multiple_of(after * win, win), win)
            out_ref[0, at, :] = out_ref[0, at, :] + jnp.where(upper, 0.0, grad)


def local(object_slices, probe_modes, prop_phase, measured, row_offsets, col_offsets, counts):
    modes, _, win, _ = probe_modes.shape
    slots = row_offsets.shape[0]
    chips = lax.axis_size("cuts") // CORES
    copies = chips // slots
    assert chips % slots == 0 and chips & (chips - 1) == 0
    section = lax.axis_index("cuts")
    chip, core = section // CORES, section % CORES
    strip = object_slices[0]
    block = jax.ShapeDtypeStruct((2, win, win), BF16)
    order = sorted(range(1, chips), reverse=True)
    near, far = list(range(chips // 2)), [p for p in order if p >= chips // 2]

    def joined(blocks, group):
        return jnp.concatenate([blocks[p] for p in group], 0) if len(group) > 1 else blocks[group[0]]


    own_strip = strip.astype(BF16)
    beside = passed_round(own_strip, "tile", -1)
    tile = lax.axis_index("tile")
    rightmost = tile == lax.axis_size("tile") - 1
    ints = jnp.stack([chip, core, rightmost]).astype(jnp.int32)
    slot = chip // copies
    place = jnp.stack([row_offsets[slot], col_offsets[slot]])
    probe = pl.pallas_call(
        functools.partial(rolled_probe_kernel, win),
        out_shape=jax.ShapeDtypeStruct(probe_modes.shape, BF16),
        in_specs=[SMEM, VMEM],
        out_specs=VMEM,
        compiler_params=SMALL,
    )(place, probe_modes)
    matrix = dft_blocks(win)
    left_matrix = jnp.asarray(matrix, BF16)
    right_matrix = jnp.asarray(matrix.T, BF16)
    unit = 1.0 / (ENTRY_SCALE * ENTRY_SCALE * win)
    hcos = jnp.cos(prop_phase) * (unit * unit)
    hsin = jnp.sin(prop_phase) * (unit * unit)
    target = lax.dynamic_index_in_dim(measured, slot, 0, keepdims=False)
    weight = (slot < counts).astype(F32)

    note = jnp.stack([row_offsets // win, row_offsets % win, col_offsets]).astype(BF16)
    note = jnp.pad(note, ((0, 16 - 3), (0, win - slots)))
    beside, probe, hcos, hsin, target, weight, note = lax.optimization_barrier(
        (beside, probe, hcos, hsin, target, weight, note)
    )
    merged = pl.pallas_call(
        functools.partial(merge_kernel, chips, slots, win),
        out_shape=[block] * chips,
        in_specs=[SMEM, SMEM, SMEM, VMEM, VMEM],
        out_specs=[VMEM] * chips,
        compiler_params=SMALL,
    )(ints, row_offsets, col_offsets, own_strip, beside)
    own_blocks = [merged[0]] + [None] * (chips - 1)
    for p in order:
        own_blocks[p] = crossed(merged[p], p)
    swaps = [[p] for p in order] + [[0]]
    other_blocks = [swapped(joined(own_blocks, group)) for group in swaps]

    grads = pl.pallas_call(
        functools.partial(window_kernel, chips, modes, win, swaps),
        out_shape=[block] * chips,
        in_specs=[SMEM, SMEM] + [VMEM] * (6 + chips + len(swaps)),
        out_specs=[VMEM] * chips,
        scratch_shapes=[
            pltpu.VMEM((CORES * chips, 2, win, win), BF16),
            pltpu.VMEM((CORES * chips, modes, 2, win, win), F32),
            pltpu.VMEM((CORES * chips, 2, win, win), BF16),
        ],
        compiler_params=LARGE,
    )(ints, weight, left_matrix, right_matrix, probe, hcos, hsin, target, *own_blocks[::-1], *other_blocks)

    mine = [grads[0]] + [None] * (chips - 1)
    for p in order:
        mine[p] = crossed(grads[p], p)
    for p in near[1:]:
        mine[p], mine[far[-1]] = lax.optimization_barrier((mine[p], mine[far[-1]]))
    size = len(near) * 2 * win
    first = jnp.concatenate([mine[p].reshape(2 * win, win) for p in near] + [note], 0)
    first = passed_round(first, "tile", 1)
    places = first[size : size + 3, :slots].astype(jnp.int32)
    left_rows, left_cols = places[0] * win + places[1], jnp.where(tile > 0, places[2], 0)
    groups = [near, far]
    wrapped = [first[:size].reshape(-1, win, win), passed_round(joined(mine, far), "tile", 1)]

    def placed(groups, from_left, rows, cols, *arrays):
        return pl.pallas_call(
            functools.partial(place_kernel, chips, slots, win, groups, from_left),
            out_shape=jax.ShapeDtypeStruct(strip.shape, F32),
            grid=(2,),
            in_specs=[SMEM, SMEM, SMEM] + [VMEM] * len(arrays),
            out_specs=pl.BlockSpec((1,) + strip.shape[1:], lambda part: (part, 0, 0)),
            compiler_params=SMALL,
        )(ints, rows, cols, *arrays)

    own_part = placed([[p] for p in range(chips)], False, row_offsets, col_offsets, *mine)
    return placed(groups, True, left_rows, left_cols, *wrapped, own_part)[None]


def solution(mesh):
    placed = (
        P("cuts", None, None, "tile"),
        P(),
        P(),
        P("tile", None, None),
        P("tile"),
        P("tile"),
        P("tile"),
    )
    return jax.shard_map(
        local, mesh=mesh, in_specs=placed, out_specs=P("cuts", None, None, "tile"), check_vma=False
    )
```

```python
import functools
import math

import jax
import jax.numpy as jnp
import numpy as np
from jax import lax
from jax.experimental import pallas as pl
from jax.experimental.pallas import tpu as pltpu
from jax.sharding import PartitionSpec as P

F32 = jnp.float32
BF16 = jnp.bfloat16
CORES = 2
ENTRY_SCALE = 1.62475

VMEM = pl.BlockSpec(memory_space=pltpu.VMEM)
SMEM = pl.BlockSpec(memory_space=pltpu.SMEM)
SMALL = pltpu.CompilerParams(vmem_limit_bytes=8 * 2**20)
LARGE = pltpu.CompilerParams(vmem_limit_bytes=24 * 2**20)


def passed_round(block, axis, distance):
    size = lax.axis_size(axis)
    return lax.ppermute(block, axis, [(i, (i + distance) % size) for i in range(size)])


def crossed(block, distance):
    size = lax.axis_size("cuts")
    return lax.ppermute(block, "cuts", [(i, i ^ (CORES * distance)) for i in range(size)])


def swapped(block):
    size = lax.axis_size("cuts")
    return lax.ppermute(block, "cuts", [(i, i ^ 1) for i in range(size)])


def dft_blocks(win):
    numbers = np.arange(win)
    angles = (numbers[:, None] * numbers[None, :] % win) * (2.0 * math.pi / win)
    cosine, sine = np.cos(angles) * ENTRY_SCALE, np.sin(angles) * ENTRY_SCALE
    return np.block([[cosine, sine], [-sine, cosine]]).astype(np.float32)


def merge_kernel(chips, slots, win, ints_ref, rows_ref, cols_ref, own_ref, beside_ref, *out_refs):
    row_ids = lax.broadcasted_iota(jnp.int32, (win, win), 0)
    col_ids = lax.broadcasted_iota(jnp.int32, (win, win), 1)
    last = own_ref.shape[1] // win - 1
    inside = ints_ref[2] == 0

    def columns(part, at, mine):
        beside = jnp.where(inside, beside_ref[part, at, :].astype(F32), 0.0)
        return jnp.where(mine, own_ref[part, at, :].astype(F32), beside)

    for p in range(chips):
        slot = (ints_ref[0] ^ p) // (chips // slots)
        row_at, col_at = rows_ref[slot], cols_ref[slot]
        block = row_at // win
        after = jnp.minimum(block + 1, last)
        upper = row_ids >= row_at - block * win
        mine = col_ids >= col_at
        for part in range(2):
            at = pl.ds(pl.multiple_of(block * win, win), win)
            first = columns(part, at, mine)
            at = pl.ds(pl.multiple_of(after * win, win), win)
            second = columns(part, at, mine)
            out_refs[p][part] = jnp.where(upper, first, second).astype(BF16)


def rolled_probe_kernel(win, place_ref, probe_ref, out_ref):
    row_at, col_at = lax.rem(place_ref[0], win), place_ref[1]
    for mode in range(probe_ref.shape[0]):
        for part in range(2):
            block = pltpu.roll(probe_ref[mode, part], row_at, 0)
            out_ref[mode, part] = pltpu.roll(block, col_at, 1).astype(BF16)


def window_kernel(chips, modes, win, groups, *refs):
    slices = CORES * chips
    (ints_ref, weight_ref, left_ref, right_ref, probe_ref, hcos_ref, hsin_ref, target_ref) = refs[:8]
    own_refs = refs[8 : 8 + chips]
    refs = refs[8 + chips :]
    other_refs, refs = refs[: len(groups)], refs[len(groups) :]
    out_refs, (patch_ref, wave_ref, grad_ref) = refs[:chips], refs[chips:]
    chip, core = ints_ref[0], ints_ref[1]
    unit = 1.0 / (ENTRY_SCALE * ENTRY_SCALE * win)
    for p, own_ref in zip(reversed(range(chips)), own_refs):
        patch_ref[CORES * (chip ^ p) + core] = own_ref[...]
    for other_ref, group in zip(other_refs, groups):
        for place, p in enumerate(group):
            patch_ref[CORES * (chip ^ p) + 1 - core] = other_ref[2 * place : 2 * place + 2]

    def from_left(matrix, pairs):
        stacked = jnp.concatenate(
            [jnp.concatenate([pair[k].astype(BF16) for pair in pairs], 1) for k in range(2)], 0
        )
        prod = jnp.dot(matrix, stacked, preferred_element_type=F32)
        return [
            (prod[:win, m * win : (m + 1) * win], prod[win:, m * win : (m + 1) * win])
            for m in range(modes)
        ]

    def from_right(pairs, matrix):
        stacked = jnp.concatenate(
            [jnp.concatenate([pair[k].astype(BF16) for k in range(2)], 1) for pair in pairs], 0
        )
        prod = jnp.dot(stacked, matrix, preferred_element_type=F32)
        return [
            (prod[m * win : (m + 1) * win, :win], prod[m * win : (m + 1) * win, win:])
            for m in range(modes)
        ]

    def transform(pairs):
        return from_right(from_left(left_ref[...], pairs), right_ref[...])

    def inverse(pairs):
        return from_left(right_ref[...], from_right(pairs, left_ref[...]))

    def mul(a, b):
        return (a[0] * b[0] - a[1] * b[1], a[0] * b[1] + a[1] * b[0])

    def conj_mul(a, b):
        return (a[0] * b[0] + a[1] * b[1], a[0] * b[1] - a[1] * b[0])

    def patch_at(s):
        return (patch_ref[s, 0].astype(F32), patch_ref[s, 1].astype(F32))

    def waves_at(s):
        return [(wave_ref[s, m, 0], wave_ref[s, m, 1]) for m in range(modes)]

    def propagator():
        return (hcos_ref[...], hsin_ref[...])

    for m in range(modes):
        for part in range(2):
            wave_ref[0, m, part] = probe_ref[m, part].astype(F32)

    def forward_step(s, carry):
        patch = patch_at(s)
        freq = transform([mul(wave, patch) for wave in waves_at(s)])
        spread = propagator()
        waves = inverse([mul(spread, pair) for pair in freq])
        for m in range(modes):
            for part in range(2):
                wave_ref[s + 1, m, part] = waves[m][part]
        return carry

    lax.fori_loop(0, slices - 1, forward_step, 0, unroll=True)
    patch = patch_at(slices - 1)
    exits = transform([mul(wave, patch) for wave in waves_at(slices - 1)])
    power = sum(pair[0] * pair[0] + pair[1] * pair[1] for pair in exits) * (unit * unit)
    factor = (power - target_ref[...]) * (weight_ref[0] * (0.25 * unit * unit))
    back = inverse([(factor * pair[0], factor * pair[1]) for pair in exits])

    def keep_grad(s, back):
        grads = [conj_mul(wave, pair) for wave, pair in zip(waves_at(s), back)]
        for part in range(2):
            grad_ref[s, part] = sum(grad[part] for grad in grads).astype(BF16)

    keep_grad(slices - 1, back)

    def backward_step(i, back):
        s = slices - 1 - i
        patch = patch_at(s)
        freq = transform([conj_mul(patch, pair) for pair in back])
        spread = propagator()
        back = inverse([conj_mul(spread, pair) for pair in freq])
        keep_grad(s - 1, back)
        return back

    lax.fori_loop(0, slices - 1, backward_step, back, unroll=True)
    for p in range(chips):
        out_refs[p][...] = grad_ref[CORES * (chip ^ p) + core]


def place_kernel(chips, slots, win, groups, from_left, *refs):
    chip_ref, rows_ref, cols_ref = refs[:3]
    block_refs = refs[3 : 3 + len(groups)]
    out_ref = refs[-1]
    part = pl.program_id(0)
    if from_left:
        out_ref[0] = refs[3 + len(groups)][part]
    else:
        out_ref[...] = jnp.zeros_like(out_ref)
    row_ids = lax.broadcasted_iota(jnp.int32, (win, win), 0)
    col_ids = lax.broadcasted_iota(jnp.int32, (win, win), 1)
    last = out_ref.shape[1] // win - 1
    copies = chips // slots
    for block_ref, group in zip(block_refs, groups):
        for place, p in enumerate(group):
            source = chip_ref[0] ^ p
            slot = source // copies
            row_at, col_at = rows_ref[slot], cols_ref[slot]
            mine = (col_ids < col_at) if from_left else (col_ids >= col_at)
            counted = lax.rem(source, copies) == 0
            block = row_at // win
            after = jnp.minimum(block + 1, last)
            upper = row_ids >= row_at - block * win
            grad = jnp.where(mine & counted, block_ref[2 * place + part].astype(F32), 0.0)
            at = pl.ds(pl.multiple_of(block * win, win), win)
            out_ref[0, at, :] = out_ref[0, at, :] + jnp.where(upper, grad, 0.0)
            at = pl.ds(pl.multiple_of(after * win, win), win)
            out_ref[0, at, :] = out_ref[0, at, :] + jnp.where(upper, 0.0, grad)


def local(object_slices, probe_modes, prop_phase, measured, row_offsets, col_offsets, counts):
    modes, _, win, _ = probe_modes.shape
    slots = row_offsets.shape[0]
    chips = lax.axis_size("cuts") // CORES
    copies = chips // slots
    assert chips % slots == 0 and chips & (chips - 1) == 0
    section = lax.axis_index("cuts")
    chip, core = section // CORES, section % CORES
    strip = object_slices[0]
    block = jax.ShapeDtypeStruct((2, win, win), BF16)
    order = sorted(range(1, chips), reverse=True)
    near, far = list(range(chips // 2)), [p for p in order if p >= chips // 2]

    def joined(blocks, group):
        return jnp.concatenate([blocks[p] for p in group], 0) if len(group) > 1 else blocks[group[0]]


    own_strip = strip.astype(BF16)
    beside = passed_round(own_strip, "tile", -1)
    tile = lax.axis_index("tile")
    rightmost = tile == lax.axis_size("tile") - 1
    ints = jnp.stack([chip, core, rightmost]).astype(jnp.int32)
    slot = chip // copies
    place = jnp.stack([row_offsets[slot], col_offsets[slot]])
    probe = pl.pallas_call(
        functools.partial(rolled_probe_kernel, win),
        out_shape=jax.ShapeDtypeStruct(probe_modes.shape, BF16),
        in_specs=[SMEM, VMEM],
        out_specs=VMEM,
        compiler_params=SMALL,
    )(place, probe_modes)
    matrix = dft_blocks(win)
    left_matrix = jnp.asarray(matrix, BF16)
    right_matrix = jnp.asarray(matrix.T, BF16)
    unit = 1.0 / (ENTRY_SCALE * ENTRY_SCALE * win)
    hcos = jnp.cos(prop_phase) * (unit * unit)
    hsin = jnp.sin(prop_phase) * (unit * unit)
    target = lax.dynamic_index_in_dim(measured, slot, 0, keepdims=False)
    weight = (slot < counts).astype(F32)

    note = jnp.stack([row_offsets // win, row_offsets % win, col_offsets]).astype(BF16)
    note = jnp.pad(note, ((0, 16 - 3), (0, win - slots)))
    beside, probe, hcos, hsin, target, weight, note = lax.optimization_barrier(
        (beside, probe, hcos, hsin, target, weight, note)
    )
    merged = pl.pallas_call(
        functools.partial(merge_kernel, chips, slots, win),
        out_shape=[block] * chips,
        in_specs=[SMEM, SMEM, SMEM, VMEM, VMEM],
        out_specs=[VMEM] * chips,
        compiler_params=SMALL,
    )(ints, row_offsets, col_offsets, own_strip, beside)
    own_blocks = [merged[0]] + [None] * (chips - 1)
    for p in order:
        own_blocks[p] = crossed(merged[p], p)
    swaps = [[p] for p in order] + [[0]]
    other_blocks = [swapped(joined(own_blocks, group)) for group in swaps]

    grads = pl.pallas_call(
        functools.partial(window_kernel, chips, modes, win, swaps),
        out_shape=[block] * chips,
        in_specs=[SMEM, SMEM] + [VMEM] * (6 + chips + len(swaps)),
        out_specs=[VMEM] * chips,
        scratch_shapes=[
            pltpu.VMEM((CORES * chips, 2, win, win), BF16),
            pltpu.VMEM((CORES * chips, modes, 2, win, win), F32),
            pltpu.VMEM((CORES * chips, 2, win, win), BF16),
        ],
        compiler_params=LARGE,
    )(ints, weight, left_matrix, right_matrix, probe, hcos, hsin, target, *own_blocks[::-1], *other_blocks)

    mine = [grads[0]] + [None] * (chips - 1)
    for p in order:
        mine[p] = crossed(grads[p], p)
    far = far[::-1]
    size = len(near) * 2 * win
    first = jnp.concatenate([mine[p].reshape(2 * win, win) for p in near] + [note], 0)
    first = passed_round(first, "tile", 1)
    places = first[size : size + 3, :slots].astype(jnp.int32)
    left_rows, left_cols = places[0] * win + places[1], jnp.where(tile > 0, places[2], 0)
    groups = [near, far]
    wrapped = [first[:size].reshape(-1, win, win), passed_round(joined(mine, far), "tile", 1)]

    def placed(groups, from_left, rows, cols, *arrays):
        return pl.pallas_call(
            functools.partial(place_kernel, chips, slots, win, groups, from_left),
            out_shape=jax.ShapeDtypeStruct(strip.shape, F32),
            grid=(2,),
            in_specs=[SMEM, SMEM, SMEM] + [VMEM] * len(arrays),
            out_specs=pl.BlockSpec((1,) + strip.shape[1:], lambda part: (part, 0, 0)),
            compiler_params=SMALL,
        )(ints, rows, cols, *arrays)

    own_part = placed([[p] for p in range(chips)], False, row_offsets, col_offsets, *mine)
    return placed(groups, True, left_rows, left_cols, *wrapped, own_part)[None]


def solution(mesh):
    placed = (
        P("cuts", None, None, "tile"),
        P(),
        P(),
        P("tile", None, None),
        P("tile"),
        P("tile"),
        P("tile"),
    )
    return jax.shard_map(
        local, mesh=mesh, in_specs=placed, out_specs=P("cuts", None, None, "tile"), check_vma=False
    )
```

```python
import functools
import math

import jax
import jax.numpy as jnp
import numpy as np
from jax import lax
from jax.experimental import pallas as pl
from jax.experimental.pallas import tpu as pltpu
from jax.sharding import PartitionSpec as P

F32 = jnp.float32
BF16 = jnp.bfloat16
CORES = 2
ENTRY_SCALE = 1.62475

VMEM = pl.BlockSpec(memory_space=pltpu.VMEM)
SMEM = pl.BlockSpec(memory_space=pltpu.SMEM)
SMALL = pltpu.CompilerParams(vmem_limit_bytes=8 * 2**20)
LARGE = pltpu.CompilerParams(vmem_limit_bytes=24 * 2**20)


def passed_round(block, axis, distance):
    size = lax.axis_size(axis)
    return lax.ppermute(block, axis, [(i, (i + distance) % size) for i in range(size)])


def crossed(block, distance):
    size = lax.axis_size("cuts")
    return lax.ppermute(block, "cuts", [(i, i ^ (CORES * distance)) for i in range(size)])


def swapped(block):
    size = lax.axis_size("cuts")
    return lax.ppermute(block, "cuts", [(i, i ^ 1) for i in range(size)])


def dft_blocks(win):
    numbers = np.arange(win)
    angles = (numbers[:, None] * numbers[None, :] % win) * (2.0 * math.pi / win)
    cosine, sine = np.cos(angles) * ENTRY_SCALE, np.sin(angles) * ENTRY_SCALE
    return np.block([[cosine, sine], [-sine, cosine]]).astype(np.float32)


def merge_kernel(chips, slots, win, ints_ref, rows_ref, cols_ref, own_ref, beside_ref, *out_refs):
    row_ids = lax.broadcasted_iota(jnp.int32, (win, win), 0)
    col_ids = lax.broadcasted_iota(jnp.int32, (win, win), 1)
    last = own_ref.shape[1] // win - 1
    inside = ints_ref[2] == 0

    def columns(part, at, mine):
        beside = jnp.where(inside, beside_ref[part, at, :].astype(F32), 0.0)
        return jnp.where(mine, own_ref[part, at, :].astype(F32), beside)

    for p in range(chips):
        slot = (ints_ref[0] ^ p) // (chips // slots)
        row_at, col_at = rows_ref[slot], cols_ref[slot]
        block = row_at // win
        after = jnp.minimum(block + 1, last)
        upper = row_ids >= row_at - block * win
        mine = col_ids >= col_at
        for part in range(2):
            at = pl.ds(pl.multiple_of(block * win, win), win)
            first = columns(part, at, mine)
            at = pl.ds(pl.multiple_of(after * win, win), win)
            second = columns(part, at, mine)
            out_refs[p][part] = jnp.where(upper, first, second).astype(BF16)


def rolled_probe_kernel(win, place_ref, probe_ref, out_ref):
    row_at, col_at = lax.rem(place_ref[0], win), place_ref[1]
    for mode in range(probe_ref.shape[0]):
        for part in range(2):
            block = pltpu.roll(probe_ref[mode, part], row_at, 0)
            out_ref[mode, part] = pltpu.roll(block, col_at, 1).astype(BF16)


def window_kernel(chips, modes, win, groups, *refs):
    slices = CORES * chips
    (ints_ref, weight_ref, left_ref, right_ref, probe_ref, hcos_ref, hsin_ref, target_ref) = refs[:8]
    own_refs = refs[8 : 8 + chips]
    refs = refs[8 + chips :]
    other_refs, refs = refs[: len(groups)], refs[len(groups) :]
    out_refs, (patch_ref, wave_ref, grad_ref) = refs[:chips], refs[chips:]
    chip, core = ints_ref[0], ints_ref[1]
    unit = 1.0 / (ENTRY_SCALE * ENTRY_SCALE * win)
    for p, own_ref in zip(reversed(range(chips)), own_refs):
        patch_ref[CORES * (chip ^ p) + core] = own_ref[...]
    for other_ref, group in zip(other_refs, groups):
        for place, p in enumerate(group):
            patch_ref[CORES * (chip ^ p) + 1 - core] = other_ref[2 * place : 2 * place + 2]

    def from_left(matrix, pairs):
        stacked = jnp.concatenate(
            [jnp.concatenate([pair[k].astype(BF16) for pair in pairs], 1) for k in range(2)], 0
        )
        prod = jnp.concatenate(
            [
                jnp.concatenate(
                    [
                        jnp.dot(rows, stacked[:, at : at + win], preferred_element_type=F32)
                        for rows in (matrix[:win], matrix[win:])
                    ],
                    0,
                )
                for at in range(0, modes * win, win)
            ],
            1,
        )
        return [
            (prod[:win, m * win : (m + 1) * win], prod[win:, m * win : (m + 1) * win])
            for m in range(modes)
        ]

    def from_right(pairs, matrix):
        prods = [
            jnp.dot(
                jnp.concatenate([pair[k].astype(BF16) for k in range(2)], 1),
                matrix,
                preferred_element_type=F32,
            )
            for pair in pairs
        ]
        return [(prod[:, :win], prod[:, win:]) for prod in prods]

    def transform(pairs):
        return from_right(from_left(left_ref[...], pairs), right_ref[...])

    def inverse(pairs):
        return from_left(right_ref[...], from_right(pairs, left_ref[...]))

    def mul(a, b):
        return (a[0] * b[0] - a[1] * b[1], a[0] * b[1] + a[1] * b[0])

    def conj_mul(a, b):
        return (a[0] * b[0] + a[1] * b[1], a[0] * b[1] - a[1] * b[0])

    def patch_at(s):
        return (patch_ref[s, 0].astype(F32), patch_ref[s, 1].astype(F32))

    def waves_at(s):
        return [(wave_ref[s, m, 0], wave_ref[s, m, 1]) for m in range(modes)]

    def propagator():
        return (hcos_ref[...], hsin_ref[...])

    for m in range(modes):
        for part in range(2):
            wave_ref[0, m, part] = probe_ref[m, part].astype(F32)

    def forward_step(s, carry):
        patch = patch_at(s)
        freq = transform([mul(wave, patch) for wave in waves_at(s)])
        spread = propagator()
        waves = inverse([mul(spread, pair) for pair in freq])
        for m in range(modes):
            for part in range(2):
                wave_ref[s + 1, m, part] = waves[m][part]
        return carry

    lax.fori_loop(0, slices - 1, forward_step, 0, unroll=True)
    patch = patch_at(slices - 1)
    exits = transform([mul(wave, patch) for wave in waves_at(slices - 1)])
    power = sum(pair[0] * pair[0] + pair[1] * pair[1] for pair in exits) * (unit * unit)
    factor = (power - target_ref[...]) * (weight_ref[0] * (0.25 * unit * unit))
    back = inverse([(factor * pair[0], factor * pair[1]) for pair in exits])

    def keep_grad(s, back):
        grads = [conj_mul(wave, pair) for wave, pair in zip(waves_at(s), back)]
        for part in range(2):
            grad_ref[s, part] = sum(grad[part] for grad in grads).astype(BF16)

    keep_grad(slices - 1, back)

    def backward_step(i, back):
        s = slices - 1 - i
        patch = patch_at(s)
        freq = transform([conj_mul(patch, pair) for pair in back])
        spread = propagator()
        back = inverse([conj_mul(spread, pair) for pair in freq])
        keep_grad(s - 1, back)
        return back

    lax.fori_loop(0, slices - 1, backward_step, back, unroll=True)
    for p in range(chips):
        out_refs[p][...] = grad_ref[CORES * (chip ^ p) + core]


def place_kernel(chips, slots, win, groups, from_left, *refs):
    chip_ref, rows_ref, cols_ref = refs[:3]
    block_refs = refs[3 : 3 + len(groups)]
    out_ref = refs[-1]
    part = pl.program_id(0)
    if from_left:
        out_ref[0] = refs[3 + len(groups)][part]
    else:
        out_ref[...] = jnp.zeros_like(out_ref)
    row_ids = lax.broadcasted_iota(jnp.int32, (win, win), 0)
    col_ids = lax.broadcasted_iota(jnp.int32, (win, win), 1)
    last = out_ref.shape[1] // win - 1
    copies = chips // slots
    for block_ref, group in zip(block_refs, groups):
        for place, p in enumerate(group):
            source = chip_ref[0] ^ p
            slot = source // copies
            row_at, col_at = rows_ref[slot], cols_ref[slot]
            mine = (col_ids < col_at) if from_left else (col_ids >= col_at)
            counted = lax.rem(source, copies) == 0
            block = row_at // win
            after = jnp.minimum(block + 1, last)
            upper = row_ids >= row_at - block * win
            grad = jnp.where(mine & counted, block_ref[2 * place + part].astype(F32), 0.0)
            at = pl.ds(pl.multiple_of(block * win, win), win)
            out_ref[0, at, :] = out_ref[0, at, :] + jnp.where(upper, grad, 0.0)
            at = pl.ds(pl.multiple_of(after * win, win), win)
            out_ref[0, at, :] = out_ref[0, at, :] + jnp.where(upper, 0.0, grad)


def local(object_slices, probe_modes, prop_phase, measured, row_offsets, col_offsets, counts):
    modes, _, win, _ = probe_modes.shape
    slots = row_offsets.shape[0]
    chips = lax.axis_size("cuts") // CORES
    copies = chips // slots
    assert chips % slots == 0 and chips & (chips - 1) == 0
    section = lax.axis_index("cuts")
    chip, core = section // CORES, section % CORES
    strip = object_slices[0]
    block = jax.ShapeDtypeStruct((2, win, win), BF16)
    order = sorted(range(1, chips), reverse=True)
    near, far = list(range(chips // 2)), [p for p in order if p >= chips // 2]

    def joined(blocks, group):
        return jnp.concatenate([blocks[p] for p in group], 0) if len(group) > 1 else blocks[group[0]]


    own_strip = strip.astype(BF16)
    beside = passed_round(own_strip, "tile", -1)
    tile = lax.axis_index("tile")
    rightmost = tile == lax.axis_size("tile") - 1
    ints = jnp.stack([chip, core, rightmost]).astype(jnp.int32)
    slot = chip // copies
    place = jnp.stack([row_offsets[slot], col_offsets[slot]])
    probe = pl.pallas_call(
        functools.partial(rolled_probe_kernel, win),
        out_shape=jax.ShapeDtypeStruct(probe_modes.shape, BF16),
        in_specs=[SMEM, VMEM],
        out_specs=VMEM,
        compiler_params=SMALL,
    )(place, probe_modes)
    matrix = dft_blocks(win)
    left_matrix = jnp.asarray(matrix, BF16)
    right_matrix = jnp.asarray(matrix.T, BF16)
    unit = 1.0 / (ENTRY_SCALE * ENTRY_SCALE * win)
    hcos = jnp.cos(prop_phase) * (unit * unit)
    hsin = jnp.sin(prop_phase) * (unit * unit)
    target = lax.dynamic_index_in_dim(measured, slot, 0, keepdims=False)
    weight = (slot < counts).astype(F32)

    note = jnp.stack([row_offsets // win, row_offsets % win, col_offsets]).astype(BF16)
    note = jnp.pad(note, ((0, 16 - 3), (0, win - slots)))
    beside, probe, hcos, hsin, target, weight, note = lax.optimization_barrier(
        (beside, probe, hcos, hsin, target, weight, note)
    )
    merged = pl.pallas_call(
        functools.partial(merge_kernel, chips, slots, win),
        out_shape=[block] * chips,
        in_specs=[SMEM, SMEM, SMEM, VMEM, VMEM],
        out_specs=[VMEM] * chips,
        compiler_params=SMALL,
    )(ints, row_offsets, col_offsets, own_strip, beside)
    own_blocks = [merged[0]] + [None] * (chips - 1)
    for p in order:
        own_blocks[p] = crossed(merged[p], p)
    swaps = [[p] for p in order] + [[0]]
    other_blocks = [swapped(joined(own_blocks, group)) for group in swaps]

    grads = pl.pallas_call(
        functools.partial(window_kernel, chips, modes, win, swaps),
        out_shape=[block] * chips,
        in_specs=[SMEM, SMEM] + [VMEM] * (6 + chips + len(swaps)),
        out_specs=[VMEM] * chips,
        scratch_shapes=[
            pltpu.VMEM((CORES * chips, 2, win, win), BF16),
            pltpu.VMEM((CORES * chips, modes, 2, win, win), F32),
            pltpu.VMEM((CORES * chips, 2, win, win), BF16),
        ],
        compiler_params=LARGE,
    )(ints, weight, left_matrix, right_matrix, probe, hcos, hsin, target, *own_blocks[::-1], *other_blocks)

    mine = [grads[0]] + [None] * (chips - 1)
    for p in order:
        mine[p] = crossed(grads[p], p)
    far = far[::-1]
    size = len(near) * 2 * win
    first = jnp.concatenate([mine[p].reshape(2 * win, win) for p in near] + [note], 0)
    first = passed_round(first, "tile", 1)
    places = first[size : size + 3, :slots].astype(jnp.int32)
    left_rows, left_cols = places[0] * win + places[1], jnp.where(tile > 0, places[2], 0)
    groups = [near, far]
    wrapped = [first[:size].reshape(-1, win, win), passed_round(joined(mine, far), "tile", 1)]

    def placed(groups, from_left, rows, cols, *arrays):
        return pl.pallas_call(
            functools.partial(place_kernel, chips, slots, win, groups, from_left),
            out_shape=jax.ShapeDtypeStruct(strip.shape, F32),
            grid=(2,),
            in_specs=[SMEM, SMEM, SMEM] + [VMEM] * len(arrays),
            out_specs=pl.BlockSpec((1,) + strip.shape[1:], lambda part: (part, 0, 0)),
            compiler_params=SMALL,
        )(ints, rows, cols, *arrays)

    own_part = placed([[p] for p in range(chips)], False, row_offsets, col_offsets, *mine)
    return placed(groups, True, left_rows, left_cols, *wrapped, own_part)[None]


def solution(mesh):
    placed = (
        P("cuts", None, None, "tile"),
        P(),
        P(),
        P("tile", None, None),
        P("tile"),
        P("tile"),
        P("tile"),
    )
    return jax.shard_map(
        local, mesh=mesh, in_specs=placed, out_specs=P("cuts", None, None, "tile"), check_vma=False
    )
```

```python
import functools
import math

import jax
import jax.numpy as jnp
import numpy as np
from jax import lax
from jax.experimental import pallas as pl
from jax.experimental.pallas import tpu as pltpu
from jax.sharding import PartitionSpec as P

F32 = jnp.float32
BF16 = jnp.bfloat16
CORES = 2
ENTRY_SCALE = 1.62475

VMEM = pl.BlockSpec(memory_space=pltpu.VMEM)
SMEM = pl.BlockSpec(memory_space=pltpu.SMEM)
SMALL = pltpu.CompilerParams(vmem_limit_bytes=8 * 2**20)
LARGE = pltpu.CompilerParams(vmem_limit_bytes=24 * 2**20)


def passed_round(block, axis, distance):
    size = lax.axis_size(axis)
    return lax.ppermute(block, axis, [(i, (i + distance) % size) for i in range(size)])


def crossed(block, distance):
    size = lax.axis_size("cuts")
    return lax.ppermute(block, "cuts", [(i, i ^ (CORES * distance)) for i in range(size)])


def swapped(block):
    size = lax.axis_size("cuts")
    return lax.ppermute(block, "cuts", [(i, i ^ 1) for i in range(size)])


def dft_blocks(win):
    numbers = np.arange(win)
    angles = (numbers[:, None] * numbers[None, :] % win) * (2.0 * math.pi / win)
    cosine, sine = np.cos(angles) * ENTRY_SCALE, np.sin(angles) * ENTRY_SCALE
    return np.block([[cosine, sine], [-sine, cosine]]).astype(np.float32)


def merge_kernel(chips, slots, win, ints_ref, rows_ref, cols_ref, own_ref, beside_ref, *out_refs):
    row_ids = lax.broadcasted_iota(jnp.int32, (win, win), 0)
    col_ids = lax.broadcasted_iota(jnp.int32, (win, win), 1)
    last = own_ref.shape[1] // win - 1
    inside = ints_ref[2] == 0

    def columns(part, at, mine):
        beside = jnp.where(inside, beside_ref[part, at, :].astype(F32), 0.0)
        return jnp.where(mine, own_ref[part, at, :].astype(F32), beside)

    for p in range(chips):
        slot = (ints_ref[0] ^ p) // (chips // slots)
        row_at, col_at = rows_ref[slot], cols_ref[slot]
        block = row_at // win
        after = jnp.minimum(block + 1, last)
        upper = row_ids >= row_at - block * win
        mine = col_ids >= col_at
        for part in range(2):
            at = pl.ds(pl.multiple_of(block * win, win), win)
            first = columns(part, at, mine)
            at = pl.ds(pl.multiple_of(after * win, win), win)
            second = columns(part, at, mine)
            out_refs[p][part] = jnp.where(upper, first, second).astype(BF16)


def rolled_probe_kernel(win, place_ref, probe_ref, out_ref):
    row_at, col_at = lax.rem(place_ref[0], win), place_ref[1]
    for mode in range(probe_ref.shape[0]):
        for part in range(2):
            block = pltpu.roll(probe_ref[mode, part], row_at, 0)
            out_ref[mode, part] = pltpu.roll(block, col_at, 1).astype(BF16)


def window_kernel(chips, modes, win, groups, *refs):
    slices = CORES * chips
    (ints_ref, weight_ref, left_ref, right_ref, probe_ref, hcos_ref, hsin_ref, target_ref) = refs[:8]
    own_refs = refs[8 : 8 + chips]
    refs = refs[8 + chips :]
    other_refs, refs = refs[: len(groups)], refs[len(groups) :]
    out_refs, (patch_ref, wave_ref, grad_ref) = refs[:chips], refs[chips:]
    chip, core = ints_ref[0], ints_ref[1]
    unit = 1.0 / (ENTRY_SCALE * ENTRY_SCALE * win)
    for p, own_ref in zip(reversed(range(chips)), own_refs):
        patch_ref[CORES * (chip ^ p) + core] = own_ref[...]
    for other_ref, group in zip(other_refs, groups):
        for place, p in enumerate(group):
            patch_ref[CORES * (chip ^ p) + 1 - core] = other_ref[2 * place : 2 * place + 2]

    def from_left(matrix, pairs):
        prods = []
        for pair in pairs:
            stacked = jnp.concatenate([pair[k].astype(BF16) for k in range(2)], 0)
            prods.append(
                tuple(
                    jnp.dot(rows, stacked, preferred_element_type=F32)
                    for rows in (matrix[:win], matrix[win:])
                )
            )
        return prods

    def from_right(pairs, matrix):
        prods = [
            jnp.dot(
                jnp.concatenate([pair[k].astype(BF16) for k in range(2)], 1),
                matrix,
                preferred_element_type=F32,
            )
            for pair in pairs
        ]
        return [(prod[:, :win], prod[:, win:]) for prod in prods]

    def transform(pairs):
        return from_right(from_left(left_ref[...], pairs), right_ref[...])

    def inverse(pairs):
        return from_left(right_ref[...], from_right(pairs, left_ref[...]))

    def mul(a, b):
        return (a[0] * b[0] - a[1] * b[1], a[0] * b[1] + a[1] * b[0])

    def conj_mul(a, b):
        return (a[0] * b[0] + a[1] * b[1], a[0] * b[1] - a[1] * b[0])

    def patch_at(s):
        return (patch_ref[s, 0].astype(F32), patch_ref[s, 1].astype(F32))

    def waves_at(s):
        return [(wave_ref[s, m, 0], wave_ref[s, m, 1]) for m in range(modes)]

    def propagator():
        return (hcos_ref[...], hsin_ref[...])

    for m in range(modes):
        for part in range(2):
            wave_ref[0, m, part] = probe_ref[m, part].astype(F32)

    def forward_step(s, carry):
        patch = patch_at(s)
        freq = transform(mul(wave, patch) for wave in waves_at(s))
        spread = propagator()
        waves = inverse(mul(spread, pair) for pair in freq)
        for m in range(modes):
            for part in range(2):
                wave_ref[s + 1, m, part] = waves[m][part]
        return carry

    lax.fori_loop(0, slices - 1, forward_step, 0, unroll=True)
    patch = patch_at(slices - 1)
    exits = transform(mul(wave, patch) for wave in waves_at(slices - 1))
    power = sum(pair[0] * pair[0] + pair[1] * pair[1] for pair in exits) * (unit * unit)
    factor = (power - target_ref[...]) * (weight_ref[0] * (0.25 * unit * unit))
    back = inverse((factor * pair[0], factor * pair[1]) for pair in exits)

    def keep_grad(s, back):
        grads = [conj_mul(wave, pair) for wave, pair in zip(waves_at(s), back)]
        for part in range(2):
            grad_ref[s, part] = sum(grad[part] for grad in grads).astype(BF16)

    keep_grad(slices - 1, back)

    def backward_step(i, back):
        s = slices - 1 - i
        patch = patch_at(s)
        freq = transform(conj_mul(patch, pair) for pair in back)
        spread = propagator()
        back = inverse(conj_mul(spread, pair) for pair in freq)
        keep_grad(s - 1, back)
        return back

    lax.fori_loop(0, slices - 1, backward_step, back, unroll=True)
    for p in range(chips):
        out_refs[p][...] = grad_ref[CORES * (chip ^ p) + core]


def place_kernel(chips, slots, win, groups, from_left, *refs):
    chip_ref, rows_ref, cols_ref = refs[:3]
    block_refs = refs[3 : 3 + len(groups)]
    out_ref = refs[-1]
    part = pl.program_id(0)
    if from_left:
        out_ref[0] = refs[3 + len(groups)][part]
    else:
        out_ref[...] = jnp.zeros_like(out_ref)
    row_ids = lax.broadcasted_iota(jnp.int32, (win, win), 0)
    col_ids = lax.broadcasted_iota(jnp.int32, (win, win), 1)
    last = out_ref.shape[1] // win - 1
    copies = chips // slots
    for block_ref, group in zip(block_refs, groups):
        for place, p in enumerate(group):
            source = chip_ref[0] ^ p
            slot = source // copies
            row_at, col_at = rows_ref[slot], cols_ref[slot]
            mine = (col_ids < col_at) if from_left else (col_ids >= col_at)
            counted = lax.rem(source, copies) == 0
            block = row_at // win
            after = jnp.minimum(block + 1, last)
            upper = row_ids >= row_at - block * win
            grad = jnp.where(mine & counted, block_ref[2 * place + part].astype(F32), 0.0)
            at = pl.ds(pl.multiple_of(block * win, win), win)
            out_ref[0, at, :] = out_ref[0, at, :] + jnp.where(upper, grad, 0.0)
            at = pl.ds(pl.multiple_of(after * win, win), win)
            out_ref[0, at, :] = out_ref[0, at, :] + jnp.where(upper, 0.0, grad)


def local(object_slices, probe_modes, prop_phase, measured, row_offsets, col_offsets, counts):
    modes, _, win, _ = probe_modes.shape
    slots = row_offsets.shape[0]
    chips = lax.axis_size("cuts") // CORES
    copies = chips // slots
    assert chips % slots == 0 and chips & (chips - 1) == 0
    section = lax.axis_index("cuts")
    chip, core = section // CORES, section % CORES
    strip = object_slices[0]
    block = jax.ShapeDtypeStruct((2, win, win), BF16)
    order = sorted(range(1, chips), reverse=True)
    near, far = list(range(chips // 2)), [p for p in order if p >= chips // 2]

    def joined(blocks, group):
        return jnp.concatenate([blocks[p] for p in group], 0) if len(group) > 1 else blocks[group[0]]


    own_strip = strip.astype(BF16)
    beside = passed_round(own_strip, "tile", -1)
    tile = lax.axis_index("tile")
    rightmost = tile == lax.axis_size("tile") - 1
    ints = jnp.stack([chip, core, rightmost]).astype(jnp.int32)
    slot = chip // copies
    place = jnp.stack([row_offsets[slot], col_offsets[slot]])
    probe = pl.pallas_call(
        functools.partial(rolled_probe_kernel, win),
        out_shape=jax.ShapeDtypeStruct(probe_modes.shape, BF16),
        in_specs=[SMEM, VMEM],
        out_specs=VMEM,
        compiler_params=SMALL,
    )(place, probe_modes)
    matrix = dft_blocks(win)
    left_matrix = jnp.asarray(matrix, BF16)
    right_matrix = jnp.asarray(matrix.T, BF16)
    unit = 1.0 / (ENTRY_SCALE * ENTRY_SCALE * win)
    hcos = jnp.cos(prop_phase) * (unit * unit)
    hsin = jnp.sin(prop_phase) * (unit * unit)
    target = lax.dynamic_index_in_dim(measured, slot, 0, keepdims=False)
    weight = (slot < counts).astype(F32)

    note = jnp.stack([row_offsets // win, row_offsets % win, col_offsets]).astype(BF16)
    note = jnp.pad(note, ((0, 16 - 3), (0, win - slots)))
    beside, probe, hcos, hsin, target, weight, note = lax.optimization_barrier(
        (beside, probe, hcos, hsin, target, weight, note)
    )
    merged = pl.pallas_call(
        functools.partial(merge_kernel, chips, slots, win),
        out_shape=[block] * chips,
        in_specs=[SMEM, SMEM, SMEM, VMEM, VMEM],
        out_specs=[VMEM] * chips,
        compiler_params=SMALL,
    )(ints, row_offsets, col_offsets, own_strip, beside)
    own_blocks = [merged[0]] + [None] * (chips - 1)
    for p in order:
        own_blocks[p] = crossed(merged[p], p)
    swaps = [[p] for p in order] + [[0]]
    other_blocks = [swapped(joined(own_blocks, group)) for group in swaps]

    grads = pl.pallas_call(
        functools.partial(window_kernel, chips, modes, win, swaps),
        out_shape=[block] * chips,
        in_specs=[SMEM, SMEM] + [VMEM] * (6 + chips + len(swaps)),
        out_specs=[VMEM] * chips,
        scratch_shapes=[
            pltpu.VMEM((CORES * chips, 2, win, win), BF16),
            pltpu.VMEM((CORES * chips, modes, 2, win, win), F32),
            pltpu.VMEM((CORES * chips, 2, win, win), BF16),
        ],
        compiler_params=LARGE,
    )(ints, weight, left_matrix, right_matrix, probe, hcos, hsin, target, *own_blocks[::-1], *other_blocks)

    mine = [grads[0]] + [None] * (chips - 1)
    for p in order:
        mine[p] = crossed(grads[p], p)
    far = far[::-1]
    size = len(near) * 2 * win
    first = jnp.concatenate([mine[p].reshape(2 * win, win) for p in near] + [note], 0)
    first = passed_round(first, "tile", 1)
    places = first[size : size + 3, :slots].astype(jnp.int32)
    left_rows, left_cols = places[0] * win + places[1], jnp.where(tile > 0, places[2], 0)
    groups = [near, far]
    wrapped = [first[:size].reshape(-1, win, win), passed_round(joined(mine, far), "tile", 1)]

    def placed(groups, from_left, rows, cols, *arrays):
        return pl.pallas_call(
            functools.partial(place_kernel, chips, slots, win, groups, from_left),
            out_shape=jax.ShapeDtypeStruct(strip.shape, F32),
            grid=(2,),
            in_specs=[SMEM, SMEM, SMEM] + [VMEM] * len(arrays),
            out_specs=pl.BlockSpec((1,) + strip.shape[1:], lambda part: (part, 0, 0)),
            compiler_params=SMALL,
        )(ints, rows, cols, *arrays)

    own_part = placed([[p] for p in range(chips)], False, row_offsets, col_offsets, *mine)
    return placed(groups, True, left_rows, left_cols, *wrapped, own_part)[None]


def solution(mesh):
    placed = (
        P("cuts", None, None, "tile"),
        P(),
        P(),
        P("tile", None, None),
        P("tile"),
        P("tile"),
        P("tile"),
    )
    return jax.shard_map(
        local, mesh=mesh, in_specs=placed, out_specs=P("cuts", None, None, "tile"), check_vma=False
    )
```
